512 devices in a mesh: cuts: 16 (over z_lo, x, core), space: 32 (over z_hi, y).
Axes of the slice: x: 4, y: 8, z: 8 (z_hi: 4, z_lo: 2; z = z_hi * 2 + z_lo), core: 2. Of those that a mesh axis runs over, the one named last changes fastest.
Arguments:
- start_u: float32 [16, 256, 32, 128], P('cuts', 'space'), may hold values from 0.4 to 1
- start_v: float32 [16, 256, 32, 128], P('cuts', 'space'), may hold values from 0 to 0.5
Outputs:
- next_u: float32 [16, 256, 32, 128], P('cuts', 'space')
- next_v: float32 [16, 256, 32, 128], P('cuts', 'space')
The draws below stay inside these ranges and needn't reach their ends.
All inputs are finite; a program needn't handle non-finite values.
Results may differ from the reference program's by a relative error of at most 0.00002.
Values sent between devices are 32-bit elements; how exact they have to be, the bound alone decides.
A program may use at most 64 MiB of HBM per device.

```python
import jax
import jax.numpy as jnp
from jax import lax

GY = 32
GZ = 128
COARSEN = 2
FINE_STEPS = 4
COARSE_STEPS = 2
SLICES = 16
NX = 256


def draw_start_u(key, part):
    shape = (SLICES, NX, GY, GZ)
    return jax.random.uniform(jax.random.fold_in(key, 21), shape, jnp.float32, 0.4, 1.0)


def draw_start_v(key, part):
    shape = (SLICES, NX, GY, GZ)
    return jax.random.uniform(jax.random.fold_in(key, 31), shape, jnp.float32, 0.0, 0.5)


def setup_inputs(seed: int = 0) -> dict:
    keys = jax.random.split(jax.random.key(seed), 3)
    return {
        "start_u": draw_start_u(jax.random.fold_in(keys[2], 71), 0),
        "start_v": draw_start_v(jax.random.fold_in(keys[2], 71), 0),
    }


SPREAD_FIRST = 0.14
SPREAD_SECOND = 0.13
FEED_RATE = 0.035
KILL_RATE = 0.065
COARSE_DT = 2.0


def fine_laplace(fields):
    beside_all = jnp.roll(fields, 1, 1) + jnp.roll(fields, -1, 1)
    beside_all = beside_all + jnp.roll(fields, 1, 2) + jnp.roll(fields, -1, 2)
    beside_all = beside_all + jnp.roll(fields, 1, 3) + jnp.roll(fields, -1, 3)
    return beside_all - 6.0 * fields


def reaction(fields, laplace, step_size):
    first = fields[0]
    second = fields[1]
    feeding = first * second * second
    new_first = first + step_size * (SPREAD_FIRST * laplace[0] - feeding + FEED_RATE * (1.0 - first))
    new_second = second + step_size * (SPREAD_SECOND * laplace[1] + feeding - (FEED_RATE + KILL_RATE) * second)
    return jnp.stack([new_first, new_second], axis=0)


def advance(fields):
    for sweep in range(FINE_STEPS):
        fields = reaction(fields, fine_laplace(fields), 1.0)
    return fields


def coarse_march(fields):
    factor = 1.0 / (COARSEN * COARSEN)
    for sweep in range(COARSE_STEPS):
        fields = reaction(fields, fine_laplace(fields) * factor, COARSE_DT)
    return fields


def restrict(fields):
    extent = fields.shape
    blocks = fields.reshape(2, extent[1] // COARSEN, COARSEN, extent[2] // COARSEN, COARSEN, extent[3] // COARSEN, COARSEN)
    return jnp.mean(blocks, axis=(2, 4, 6))


def prolong(coarse):
    spread = jnp.repeat(coarse, COARSEN, axis=1)
    spread = jnp.repeat(spread, COARSEN, axis=2)
    return jnp.repeat(spread, COARSEN, axis=3)


def reference(start_u, start_v):
    starts = jnp.stack([start_u, start_v], axis=1)
    finals = lax.map(advance, starts)
    start_coarse = lax.map(restrict, starts)
    end_coarse = lax.map(restrict, finals)
    predicted = lax.map(coarse_march, start_coarse)
    correction = end_coarse - predicted

    def chain_link(current, term):
        advanced = coarse_march(current) + term
        return advanced, advanced

    last_state, coarse_chain = lax.scan(chain_link, start_coarse[0], correction)
    results = finals + lax.map(prolong, coarse_chain - end_coarse)
    return results[:, 0], results[:, 1]
```

```python
import jax
import jax.numpy as jnp
from jax import lax
from jax.experimental import pallas as pl
from jax.experimental.pallas import tpu as pltpu
from jax.sharding import PartitionSpec as P

MESH = pl.DeviceIdType.MESH
GY = 32
GZ = 128
CY = GY // 2
PLANES = 8
COARSE = PLANES // 2
HALO = 4
PADDED = PLANES + 2 * HALO

SPREAD_FIRST = 0.14
SPREAD_SECOND = 0.13
FEED_RATE = 0.035
KILL_RATE = 0.065


def even_lanes(shape):
    return lax.broadcasted_iota(jnp.int32, shape, len(shape) - 1) % 2 == 0


def coarse_step(x):
    inner = x[1:-1]
    even = even_lanes(inner.shape)
    beside = x[2:] + x[:-2]
    beside = beside + pltpu.roll(inner, 1, 1) + pltpu.roll(inner, CY - 1, 1)
    beside = beside + pltpu.roll(inner, 2, 2) + pltpu.roll(inner, GZ - 2, 2)
    other = jnp.where(even, pltpu.roll(inner, GZ - 1, 2), pltpu.roll(inner, 1, 2))
    second = jnp.where(even, other, inner)
    feeding = inner * other * second
    spread = jnp.where(even, 0.5 * SPREAD_FIRST, 0.5 * SPREAD_SECOND)
    keep = jnp.where(
        even,
        1.0 - 3.0 * SPREAD_FIRST - 2.0 * FEED_RATE,
        1.0 - 3.0 * SPREAD_SECOND - 2.0 * (FEED_RATE + KILL_RATE),
    )
    gain = jnp.where(even, 2.0 * FEED_RATE, 0.0)
    sign = jnp.where(even, -2.0, 2.0)
    return keep * inner + spread * beside + gain + sign * feeding


def march(x):
    return coarse_step(coarse_step(x))


def fine_planes(source, target, first, count):
    def body(step, carry):
        p = first + step
        u = source[0, p]
        v = source[1, p]
        feeding = u * v * v
        beside = source[0, p - 1] + source[0, p + 1]
        beside = beside + pltpu.roll(u, 1, 0) + pltpu.roll(u, GY - 1, 0)
        beside = beside + pltpu.roll(u, 1, 1) + pltpu.roll(u, GZ - 1, 1)
        target[0, p] = (
            (1.0 - 6.0 * SPREAD_FIRST - FEED_RATE) * u + SPREAD_FIRST * beside + FEED_RATE - feeding
        )
        beside = source[1, p - 1] + source[1, p + 1]
        beside = beside + pltpu.roll(v, 1, 0) + pltpu.roll(v, GY - 1, 0)
        beside = beside + pltpu.roll(v, 1, 1) + pltpu.roll(v, GZ - 1, 1)
        target[1, p] = (
            (1.0 - 6.0 * SPREAD_SECOND - FEED_RATE - KILL_RATE) * v
            + SPREAD_SECOND * beside
            + feeding
        )
        return carry

    lax.fori_loop(0, count, body, 0, unroll=2)


def restrict(source, first, rows, out, count):
    def body(i, carry):
        p = first + 2 * i
        u = source[0, p] + source[0, p + 1]
        v = source[1, p] + source[1, p + 1]
        even = even_lanes(u.shape)
        rows[i] = jnp.where(even, u + pltpu.roll(u, GZ - 1, 1), v + pltpu.roll(v, 1, 1))
        out[i] = 0.125 * (rows[i, pl.ds(0, CY, stride=2)] + rows[i, pl.ds(1, CY, stride=2)])
        return carry

    lax.fori_loop(0, count, body, 0)


def kernel(
    cuts,
    space,
    u_ref,
    v_ref,
    out_u,
    out_v,
    fine,
    rows,
    start_coarse,
    end_coarse,
    mine,
    terms,
    states,
    halos,
    wings,
    fine_send,
    fine_recv,
    term_send,
    term_recv,
    halo_send,
    halo_recv,
    wing_send,
    wing_recv,
):
    n = lax.axis_index("cuts")
    s = lax.axis_index("space")
    right = {"space": lax.rem(s + 1, space)}
    left = {"space": lax.rem(s + space - 1, space)}
    rounds = cuts // 2

    barrier = pltpu.get_barrier_semaphore()
    for side in (left, right):
        pl.semaphore_signal(barrier, inc=1, device_id=side, device_id_type=MESH)
    for d in range(1, cuts):
        pl.semaphore_signal(
            barrier, inc=1, device_id={"cuts": lax.rem(n + d, cuts)}, device_id_type=MESH
        )
    pl.semaphore_wait(barrier, cuts + 1)

    def remote(source, target, send, recv, device):
        return pltpu.make_async_remote_copy(
            src_ref=source,
            dst_ref=target,
            send_sem=send,
            recv_sem=recv,
            device_id=device,
            device_id_type=MESH,
        )

    now = fine.at[0]
    copies = []
    for k, ref in enumerate((u_ref, v_ref)):
        copies.append(
            remote(
                ref.at[0, pl.ds(PLANES - HALO, HALO)],
                now.at[k, pl.ds(0, HALO)],
                fine_send.at[2 * k],
                fine_recv.at[2 * k],
                right,
            )
        )
        copies.append(
            remote(
                ref.at[0, pl.ds(0, HALO)],
                now.at[k, pl.ds(HALO + PLANES, HALO)],
                fine_send.at[2 * k + 1],
                fine_recv.at[2 * k + 1],
                left,
            )
        )
    for copy in copies:
        copy.start()
    fine[0, 0, pl.ds(HALO, PLANES)] = u_ref[0]
    fine[0, 1, pl.ds(HALO, PLANES)] = v_ref[0]
    for copy in copies:
        copy.wait()

    restrict(now, 0, rows, start_coarse, PADDED // 2)
    for t in range(4):
        fine_planes(fine.at[t % 2], fine.at[(t + 1) % 2], t + 1, PADDED - 2 - 2 * t)
    restrict(now, HALO, rows, end_coarse, COARSE)
    finish = end_coarse[...]
    correction = finish - march(start_coarse[...])
    terms[n] = jnp.where(n == 0, finish, correction)

    def term_copy(d):
        return remote(
            terms.at[n],
            terms.at[n],
            term_send.at[d],
            term_recv.at[n],
            {"cuts": lax.rem(n + d, cuts)},
        )

    for d in range(1, cuts):
        term_copy(d).start()

    def await_term(m):
        @pl.when(n != m)
        def _():
            remote(
                terms.at[m], terms.at[m], term_send.at[0], term_recv.at[m], right
            ).wait_recv()

    def halo_copies(source, r):
        return (
            remote(source, halos.at[r, 0], halo_send.at[r, 0], halo_recv.at[r, 0], right),
            remote(source, halos.at[r, 1], halo_send.at[r, 1], halo_recv.at[r, 1], left),
        )

    def wing_copies(r):
        return (
            remote(
                terms.at[2 * r, pl.ds(2, 2)],
                wings.at[r, 0],
                wing_send.at[r, 0],
                wing_recv.at[r, 0],
                right,
            ),
            remote(
                terms.at[2 * r, pl.ds(0, 2)],
                wings.at[r, 1],
                wing_send.at[r, 1],
                wing_recv.at[r, 1],
                left,
            ),
        )

    def keep(m, state):
        @pl.when(n == m)
        def _():
            mine[...] = state

    await_term(0)
    exchange = halo_copies(terms.at[0], 0)
    for copy in exchange:
        copy.start()
    keep(0, terms[0])
    await_term(2)
    for copy in wing_copies(1):
        copy.start()
    await_term(1)
    for copy in exchange:
        copy.wait()
    state = jnp.concatenate([halos[0, 0, 2:], terms[0], halos[0, 1, :2]], axis=0)
    state = march(state) + terms[1]
    states[1] = state
    keep(1, state)

    def one_round(r, carry):
        sent = halo_copies(states.at[r], r)
        for copy in sent:
            copy.start()

        @pl.when(r < rounds - 1)
        def _():
            await_term(2 * r + 2)
            for copy in wing_copies(r + 1):
                copy.start()

        await_term(2 * r + 1)
        for copy in wing_copies(r):
            copy.wait()
        for copy in sent:
            copy.wait()
        wide = jnp.concatenate([halos[r, 0], states[r], halos[r, 1]], axis=0)
        term = jnp.concatenate([wings[r, 0], terms[2 * r], wings[r, 1]], axis=0)
        wide = march(wide) + term
        keep(2 * r, wide[2:6])
        state = march(wide) + terms[2 * r + 1]
        states[r + 1] = state
        keep(2 * r + 1, state)
        return carry

    lax.fori_loop(1, rounds, one_round, 0)

    change = mine[...] - end_coarse[...]
    even = even_lanes(change.shape)
    for k, (out, spread) in enumerate(
        (
            (out_u, jnp.where(even, change, pltpu.roll(change, 1, 2))),
            (out_v, jnp.where(even, pltpu.roll(change, GZ - 1, 2), change)),
        )
    ):
        for i in range(COARSE):
            slot = k * COARSE + i
            rows[slot, pl.ds(0, CY, stride=2)] = spread[i]
            rows[slot, pl.ds(1, CY, stride=2)] = spread[i]
            added = rows[slot]
            out[0, 2 * i] = fine[0, k, HALO + 2 * i] + added
            out[0, 2 * i + 1] = fine[0, k, HALO + 2 * i + 1] + added

    for d in range(1, cuts):
        term_copy(d).wait_send()


def on_device(start_u, start_v):
    cuts = lax.axis_size("cuts")
    space = lax.axis_size("space")
    rounds = cuts // 2
    block = (COARSE, CY, GZ)
    f32 = jnp.float32
    shape = jax.ShapeDtypeStruct((1, PLANES, GY, GZ), f32)
    vmem = pl.BlockSpec(memory_space=pltpu.VMEM)
    dma = pltpu.SemaphoreType.DMA

    def body(*refs):
        kernel(cuts, space, *refs)

    return pl.pallas_call(
        body,
        out_shape=(shape, shape),
        in_specs=[vmem, vmem],
        out_specs=(vmem, vmem),
        scratch_shapes=[
            pltpu.VMEM((2, 2, PADDED, GY, GZ), f32),
            pltpu.VMEM((PADDED // 2, GY, GZ), f32),
            pltpu.VMEM((PADDED // 2, CY, GZ), f32),
            pltpu.VMEM(block, f32),
            pltpu.VMEM(block, f32),
            pltpu.VMEM((cuts, *block), f32),
            pltpu.VMEM((rounds + 1, *block), f32),
            pltpu.VMEM((rounds, 2, *block), f32),
            pltpu.VMEM((rounds, 2, 2, CY, GZ), f32),
            dma((4,)),
            dma((4,)),
            dma((cuts,)),
            dma((cuts,)),
            dma((rounds, 2)),
            dma((rounds, 2)),
            dma((rounds, 2)),
            dma((rounds, 2)),
        ],
        compiler_params=pltpu.CompilerParams(collective_id=0, has_side_effects=True),
        name="parareal",
    )(start_u, start_v)


def solution(mesh):
    return jax.shard_map(
        on_device,
        mesh=mesh,
        in_specs=(P("cuts", "space", None, None), P("cuts", "space", None, None)),
        out_specs=(P("cuts", "space", None, None), P("cuts", "space", None, None)),
        check_vma=False,
    )
```

```python
import jax
import jax.numpy as jnp
from jax import lax
from jax.experimental import pallas as pl
from jax.experimental.pallas import tpu as pltpu
from jax.sharding import PartitionSpec as P

MESH = pl.DeviceIdType.MESH
GY = 32
GZ = 128
CY = GY // 2
PLANES = 8
COARSE = PLANES // 2
HALO = 4
PADDED = PLANES + 2 * HALO

SPREAD_FIRST = 0.14
SPREAD_SECOND = 0.13
FEED_RATE = 0.035
KILL_RATE = 0.065


def even_lanes(shape):
    return lax.broadcasted_iota(jnp.int32, shape, len(shape) - 1) % 2 == 0


def coarse_step(x):
    inner = x[1:-1]
    even = even_lanes(inner.shape)
    beside = x[2:] + x[:-2]
    beside = beside + pltpu.roll(inner, 1, 1) + pltpu.roll(inner, CY - 1, 1)
    beside = beside + pltpu.roll(inner, 2, 2) + pltpu.roll(inner, GZ - 2, 2)
    other = jnp.where(even, pltpu.roll(inner, GZ - 1, 2), pltpu.roll(inner, 1, 2))
    second = jnp.where(even, other, inner)
    feeding = inner * other * second
    spread = jnp.where(even, 0.5 * SPREAD_FIRST, 0.5 * SPREAD_SECOND)
    keep = jnp.where(
        even,
        1.0 - 3.0 * SPREAD_FIRST - 2.0 * FEED_RATE,
        1.0 - 3.0 * SPREAD_SECOND - 2.0 * (FEED_RATE + KILL_RATE),
    )
    gain = jnp.where(even, 2.0 * FEED_RATE, 0.0)
    sign = jnp.where(even, -2.0, 2.0)
    return keep * inner + spread * beside + gain + sign * feeding


def march(x):
    return coarse_step(coarse_step(x))


def fine_planes(source, target, first, count):
    def body(step, carry):
        p = first + step
        u = source[0, p]
        v = source[1, p]
        feeding = u * v * v
        beside = source[0, p - 1] + source[0, p + 1]
        beside = beside + pltpu.roll(u, 1, 0) + pltpu.roll(u, GY - 1, 0)
        beside = beside + pltpu.roll(u, 1, 1) + pltpu.roll(u, GZ - 1, 1)
        target[0, p] = (
            (1.0 - 6.0 * SPREAD_FIRST - FEED_RATE) * u + SPREAD_FIRST * beside + FEED_RATE - feeding
        )
        beside = source[1, p - 1] + source[1, p + 1]
        beside = beside + pltpu.roll(v, 1, 0) + pltpu.roll(v, GY - 1, 0)
        beside = beside + pltpu.roll(v, 1, 1) + pltpu.roll(v, GZ - 1, 1)
        target[1, p] = (
            (1.0 - 6.0 * SPREAD_SECOND - FEED_RATE - KILL_RATE) * v
            + SPREAD_SECOND * beside
            + feeding
        )
        return carry

    lax.fori_loop(0, count, body, 0, unroll=2)


def restrict(source, first, rows, out, place, count):
    def body(i, carry):
        p = first + 2 * i
        u = source[0, p] + source[0, p + 1]
        v = source[1, p] + source[1, p + 1]
        even = even_lanes(u.shape)
        rows[i] = jnp.where(even, u + pltpu.roll(u, GZ - 1, 1), v + pltpu.roll(v, 1, 1))
        out[place + i] = 0.125 * (
            rows[i, pl.ds(0, CY, stride=2)] + rows[i, pl.ds(1, CY, stride=2)]
        )
        return carry

    lax.fori_loop(0, count, body, 0)


def kernel(
    cuts,
    space,
    u_ref,
    v_ref,
    out_u,
    out_v,
    fine,
    rows,
    start_coarse,
    end_coarse,
    mine,
    slots,
    wides,
    results,
    load_sem,
    fine_send,
    fine_recv,
    term_send,
    term_recv,
    first_send,
    wing_send,
    wing_recv,
    wide_send,
    wide_recv,
    result_send,
    result_recv,
):
    n = lax.axis_index("cuts")
    s = lax.axis_index("space")
    x = lax.rem(n // 2, 4)
    rounds = cuts // 4

    def at(step):
        return lax.rem(s + step + space, space)

    def seat(column, place):
        return lax.rem(place, 8) // 4 * 8 + 2 * column

    chain = n == seat(x, s)
    barrier = pltpu.get_barrier_semaphore()

    def greet(device):
        pl.semaphore_signal(barrier, inc=1, device_id=device, device_id_type=MESH)

    def remote(source, target, send, recv, device):
        return pltpu.make_async_remote_copy(
            src_ref=source,
            dst_ref=target,
            send_sem=send,
            recv_sem=recv,
            device_id=device,
            device_id_type=MESH,
        )

    greet({"space": at(-1)})
    greet({"space": at(1)})
    @pl.when(chain)
    def _():
        for d in range(1, cuts):
            greet({"cuts": lax.rem(n + d, cuts)})
        for step in (-2, -1, 1, 2):
            greet({"cuts": seat(x, at(step)), "space": at(step)})
            greet({"cuts": 0, "space": at(step)})
        for m in (1, 2):
            for step in (-1, 1):
                greet({"cuts": m, "space": at(step)})

    @pl.when(jnp.logical_not(chain))
    def _():
        greet({"cuts": seat(x, s)})

    now = fine.at[0]
    loads = []
    for k, ref in enumerate((u_ref, v_ref)):
        loads.append(
            pltpu.make_async_copy(ref.at[0], now.at[k, pl.ds(HALO, PLANES)], load_sem.at[k])
        )
    for load in loads:
        load.start()

    targets = 2 + 4 + jnp.where(chain, 4 + 3 - 1, 0)
    targets = targets + jnp.where(n == 0, 16, 0) + jnp.where((n == 1) | (n == 2), 8, 0)
    pl.semaphore_wait(barrier, targets)

    copies = []
    for k, ref in enumerate((u_ref, v_ref)):
        copies.append(
            remote(
                ref.at[0, pl.ds(PLANES - HALO, HALO)],
                now.at[k, pl.ds(0, HALO)],
                fine_send.at[2 * k],
                fine_recv.at[2 * k],
                {"space": at(1)},
            )
        )
        copies.append(
            remote(
                ref.at[0, pl.ds(0, HALO)],
                now.at[k, pl.ds(HALO + PLANES, HALO)],
                fine_send.at[2 * k + 1],
                fine_recv.at[2 * k + 1],
                {"space": at(-1)},
            )
        )
    for copy in copies:
        copy.start()
    for load in loads:
        load.wait()

    restrict(now, HALO, rows, start_coarse, 2, COARSE)
    for t in range(3):
        fine_planes(fine.at[t % 2], fine.at[(t + 1) % 2], HALO + 1 + t, PLANES - 2 - 2 * t)
    for copy in copies:
        copy.wait()
    restrict(now, 0, rows, start_coarse, 0, 2)
    restrict(now, HALO + PLANES, rows, start_coarse, COARSE + 2, 2)
    for t in range(3):
        source, target = fine.at[t % 2], fine.at[(t + 1) % 2]
        fine_planes(source, target, t + 1, HALO)
        fine_planes(source, target, PADDED - 1 - HALO - t, HALO)
    fine_planes(fine.at[1], fine.at[0], HALO, PLANES)
    restrict(now, HALO, rows, end_coarse, 0, COARSE)
    finish = end_coarse[...]
    correction = finish - march(start_coarse[...])
    slots[n, pl.ds(6, 4)] = jnp.where(n == 0, finish, correction)

    def term_copy(column):
        return remote(
            slots.at[n, pl.ds(6, 4)],
            slots.at[n, pl.ds(6, 4)],
            term_send.at[column],
            term_recv.at[n],
            {"cuts": seat(column, s)},
        )

    def wing_copy(m, source, target, width, step, side, send, column):
        return remote(
            slots.at[m, pl.ds(6 + source, width)],
            slots.at[m, pl.ds(target, width)],
            send,
            wing_recv.at[m, side],
            {"cuts": seat(column, at(step)), "space": at(step)},
        )

    wings = (
        ((0, 2, 4, 1, 0), (0, 10, 4, -1, 1), (2, 0, 2, 2, 2), (0, 14, 2, -2, 3)),
        ((0, 2, 4, 1, 0), (0, 10, 4, -1, 1)),
        ((2, 4, 2, 1, 0), (0, 10, 2, -1, 1)),
    )

    def first_wings(m):
        return [
            wing_copy(m, *wing, first_send.at[column, wing[4]], column)
            for column in range(4)
            for wing in wings[m]
        ]

    def later_wings(m, kind):
        return [wing_copy(m, *wing, wing_send.at[m, wing[4]], x) for wing in wings[kind]]

    for m in range(3):

        @pl.when(n == m)
        def _():
            for copy in first_wings(m):
                copy.start()

    for column in range(4):

        @pl.when(n != seat(column, s))
        def _():
            term_copy(column).start()

    def await_term(m):
        @pl.when(n != m)
        def _():
            own = slots.at[m, pl.ds(6, 4)]
            remote(own, own, term_send.at[0], term_recv.at[m], {"space": at(1)}).wait_recv()

    def result_copy(m):
        return remote(
            results.at[m], mine, result_send.at[m], result_recv.at[0], {"cuts": m}
        )

    def deliver(m, state):
        @pl.when((lax.rem(m // 2, 4) == x) & (m > 0))
        def _():
            results[m] = state

            @pl.when(m != n)
            def _():
                result_copy(m).start()

    def wide_copies(r):
        return [
            remote(
                wides.at[r, pl.ds(8, 4)],
                wides.at[r, pl.ds(target, 4)],
                wide_send.at[r, side],
                wide_recv.at[r, side],
                {"cuts": seat(x, at(step)), "space": at(step)},
            )
            for target, step, side in ((4, 1, 0), (12, -1, 1), (0, 2, 2), (16, -2, 3))
        ]

    def forward(base):
        for kind in range(3):
            await_term(base + kind)
            for copy in later_wings(base + kind, kind):
                copy.start()

    def three_links(base, wide, r):
        wide = march(wide) + slots[base + 1, 2:14]
        deliver(base + 1, wide[4:8])
        wide = march(wide) + slots[base + 2, 4:12]
        deliver(base + 2, wide[2:6])
        state = march(wide) + slots[base + 3, 6:10]
        wides[r + 1, pl.ds(8, 4)] = state

        @pl.when(r < rounds - 1)
        def _():
            for copy in wide_copies(r + 1):
                copy.start()

        deliver(base + 3, state)

    @pl.when(chain)
    def _():
        for m in range(4):
            await_term(m)
        for m in range(3):
            for copy in (wing_copy(m, *wing, first_send.at[0, wing[4]], x) for wing in wings[m]):
                copy.wait_recv()
        forward(4)
        three_links(0, slots[0], 0)

        def one_round(r, carry):
            base = 4 * r
            for copy in wide_copies(r):
                copy.wait()
            await_term(base + 3)
            for kind in range(3):
                for copy in later_wings(base + kind, kind):
                    copy.wait()

            @pl.when(r < rounds - 1)
            def _():
                forward(base + 4)

            wide = march(wides[r]) + slots[base]
            deliver(base, wide[6:10])
            three_links(base, wide, r)
            return carry

        lax.fori_loop(1, rounds, one_round, 0)
        for m in range(1, cuts):

            @pl.when((m // 2 % 4 == x) & (m != n))
            def _():
                result_copy(m).wait_send()

    @pl.when(n == 0)
    def _():
        mine[...] = end_coarse[...]

    @pl.when(chain & (n > 0))
    def _():
        mine[...] = results[n]

    @pl.when(jnp.logical_not(chain) & (n > 0))
    def _():
        result_copy(n).wait_recv()

    change = mine[...] - end_coarse[...]
    even = even_lanes(change.shape)
    for k, (out, spread) in enumerate(
        (
            (out_u, jnp.where(even, change, pltpu.roll(change, 1, 2))),
            (out_v, jnp.where(even, pltpu.roll(change, GZ - 1, 2), change)),
        )
    ):
        for i in range(COARSE):
            slot = k * COARSE + i
            rows[slot, pl.ds(0, CY, stride=2)] = spread[i]
            rows[slot, pl.ds(1, CY, stride=2)] = spread[i]
            added = rows[slot]
            out[0, 2 * i] = fine[0, k, HALO + 2 * i] + added
            out[0, 2 * i + 1] = fine[0, k, HALO + 2 * i + 1] + added

    for m in range(3):

        @pl.when(n == m)
        def _():
            for copy in first_wings(m):
                copy.wait_send()

    for column in range(4):

        @pl.when(n != seat(column, s))
        def _():
            term_copy(column).wait_send()


def on_device(start_u, start_v):
    cuts = lax.axis_size("cuts")
    space = lax.axis_size("space")
    rounds = cuts // 4
    block = (COARSE, CY, GZ)
    f32 = jnp.float32
    shape = jax.ShapeDtypeStruct((1, PLANES, GY, GZ), f32)
    hbm = pl.BlockSpec(memory_space=pl.ANY)
    vmem = pl.BlockSpec(memory_space=pltpu.VMEM)
    dma = pltpu.SemaphoreType.DMA

    def body(*refs):
        kernel(cuts, space, *refs)

    return pl.pallas_call(
        body,
        out_shape=(shape, shape),
        in_specs=[hbm, hbm],
        out_specs=(vmem, vmem),
        scratch_shapes=[
            pltpu.VMEM((2, 2, PADDED, GY, GZ), f32),
            pltpu.VMEM((PADDED // 2, GY, GZ), f32),
            pltpu.VMEM((PADDED // 2, CY, GZ), f32),
            pltpu.VMEM(block, f32),
            pltpu.VMEM(block, f32),
            pltpu.VMEM((cuts, 16, CY, GZ), f32),
            pltpu.VMEM((rounds + 1, 20, CY, GZ), f32),
            pltpu.VMEM((cuts, *block), f32),
            dma((2,)),
            dma((4,)),
            dma((4,)),
            dma((4,)),
            dma((cuts,)),
            dma((4, 4)),
            dma((cuts, 4)),
            dma((cuts, 4)),
            dma((rounds, 4)),
            dma((rounds, 4)),
            dma((cuts,)),
            dma((1,)),
        ],
        compiler_params=pltpu.CompilerParams(collective_id=0, has_side_effects=True),
        name="parareal",
    )(start_u, start_v)


def solution(mesh):
    return jax.shard_map(
        on_device,
        mesh=mesh,
        in_specs=(P("cuts", "space", None, None), P("cuts", "space", None, None)),
        out_specs=(P("cuts", "space", None, None), P("cuts", "space", None, None)),
        check_vma=False,
    )
```

```python
import jax
import jax.numpy as jnp
from jax import lax
from jax.experimental import pallas as pl
from jax.experimental.pallas import tpu as pltpu
from jax.sharding import PartitionSpec as P

MESH = pl.DeviceIdType.MESH
GY = 32
GZ = 128
CY = GY // 2
PLANES = 8
COARSE = PLANES // 2
HALO = 4
PADDED = PLANES + 2 * HALO

SPREAD_FIRST = 0.14
SPREAD_SECOND = 0.13
FEED_RATE = 0.035
KILL_RATE = 0.065


def even_lanes(shape):
    return lax.broadcasted_iota(jnp.int32, shape, len(shape) - 1) % 2 == 0


def coarse_step(x):
    inner = x[1:-1]
    even = even_lanes(inner.shape)
    beside = x[2:] + x[:-2]
    beside = beside + pltpu.roll(inner, 1, 1) + pltpu.roll(inner, CY - 1, 1)
    beside = beside + pltpu.roll(inner, 2, 2) + pltpu.roll(inner, GZ - 2, 2)
    other = jnp.where(even, pltpu.roll(inner, GZ - 1, 2), pltpu.roll(inner, 1, 2))
    second = jnp.where(even, other, inner)
    feeding = inner * other * second
    spread = jnp.where(even, 0.5 * SPREAD_FIRST, 0.5 * SPREAD_SECOND)
    keep = jnp.where(
        even,
        1.0 - 3.0 * SPREAD_FIRST - 2.0 * FEED_RATE,
        1.0 - 3.0 * SPREAD_SECOND - 2.0 * (FEED_RATE + KILL_RATE),
    )
    gain = jnp.where(even, 2.0 * FEED_RATE, 0.0)
    sign = jnp.where(even, -2.0, 2.0)
    return keep * inner + spread * beside + gain + sign * feeding


def march(x):
    return coarse_step(coarse_step(x))


def fine_planes(source, target, first, count):
    def body(step, carry):
        p = first + step
        u = source[0, p]
        v = source[1, p]
        feeding = u * v * v
        beside = source[0, p - 1] + source[0, p + 1]
        beside = beside + pltpu.roll(u, 1, 0) + pltpu.roll(u, GY - 1, 0)
        beside = beside + pltpu.roll(u, 1, 1) + pltpu.roll(u, GZ - 1, 1)
        target[0, p] = (
            (1.0 - 6.0 * SPREAD_FIRST - FEED_RATE) * u + SPREAD_FIRST * beside + FEED_RATE - feeding
        )
        beside = source[1, p - 1] + source[1, p + 1]
        beside = beside + pltpu.roll(v, 1, 0) + pltpu.roll(v, GY - 1, 0)
        beside = beside + pltpu.roll(v, 1, 1) + pltpu.roll(v, GZ - 1, 1)
        target[1, p] = (
            (1.0 - 6.0 * SPREAD_SECOND - FEED_RATE - KILL_RATE) * v
            + SPREAD_SECOND * beside
            + feeding
        )
        return carry

    lax.fori_loop(0, count, body, 0, unroll=2)


def restrict(source, first, rows, out, place, count):
    def body(i, carry):
        p = first + 2 * i
        u = source[0, p] + source[0, p + 1]
        v = source[1, p] + source[1, p + 1]
        even = even_lanes(u.shape)
        rows[i] = jnp.where(even, u + pltpu.roll(u, GZ - 1, 1), v + pltpu.roll(v, 1, 1))
        out[place + i] = 0.125 * (
            rows[i, pl.ds(0, CY, stride=2)] + rows[i, pl.ds(1, CY, stride=2)]
        )
        return carry

    lax.fori_loop(0, count, body, 0)


def kernel(
    cuts,
    space,
    u_ref,
    v_ref,
    out_u,
    out_v,
    fine,
    rows,
    start_coarse,
    end_coarse,
    mine,
    slots,
    wides,
    results,
    load_sem,
    fine_send,
    fine_recv,
    term_send,
    term_recv,
    first_send,
    wing_send,
    wing_recv,
    wide_send,
    wide_recv,
    result_send,
    result_recv,
):
    n = lax.axis_index("cuts")
    s = lax.axis_index("space")
    rounds = cuts // 4

    def at(step):
        return lax.rem(s + step + space, space)

    def seat(place):
        return lax.rem(place, 8) // 4 * 8

    chain = n == seat(s)
    barrier = pltpu.get_barrier_semaphore()

    def greet(device):
        pl.semaphore_signal(barrier, inc=1, device_id=device, device_id_type=MESH)

    def remote(source, target, send, recv, device):
        return pltpu.make_async_remote_copy(
            src_ref=source,
            dst_ref=target,
            send_sem=send,
            recv_sem=recv,
            device_id=device,
            device_id_type=MESH,
        )

    greet({"space": at(-1)})
    greet({"space": at(1)})
    @pl.when(chain)
    def _():
        for d in range(1, cuts):
            greet({"cuts": lax.rem(n + d, cuts)})
        for step in (-2, -1, 1, 2):
            greet({"cuts": seat(at(step)), "space": at(step)})
            greet({"cuts": 0, "space": at(step)})
        for m in (1, 2):
            for step in (-1, 1):
                greet({"cuts": m, "space": at(step)})

    @pl.when(jnp.logical_not(chain))
    def _():
        greet({"cuts": seat(s)})

    now = fine.at[0]
    loads = []
    for k, ref in enumerate((u_ref, v_ref)):
        loads.append(
            pltpu.make_async_copy(ref.at[0], now.at[k, pl.ds(HALO, PLANES)], load_sem.at[k])
        )
    for load in loads:
        load.start()

    targets = 2 + jnp.where(chain, 4 + cuts - 1, 1)
    targets = targets + jnp.where(n == 0, 4, 0) + jnp.where((n == 1) | (n == 2), 2, 0)
    pl.semaphore_wait(barrier, targets)

    copies = []
    for k, ref in enumerate((u_ref, v_ref)):
        copies.append(
            remote(
                ref.at[0, pl.ds(PLANES - HALO, HALO)],
                now.at[k, pl.ds(0, HALO)],
                fine_send.at[2 * k],
                fine_recv.at[2 * k],
                {"space": at(1)},
            )
        )
        copies.append(
            remote(
                ref.at[0, pl.ds(0, HALO)],
                now.at[k, pl.ds(HALO + PLANES, HALO)],
                fine_send.at[2 * k + 1],
                fine_recv.at[2 * k + 1],
                {"space": at(-1)},
            )
        )
    for copy in copies:
        copy.start()
    for load in loads:
        load.wait()

    restrict(now, HALO, rows, start_coarse, 2, COARSE)
    for t in range(3):
        fine_planes(fine.at[t % 2], fine.at[(t + 1) % 2], HALO + 1 + t, PLANES - 2 - 2 * t)
    for copy in copies:
        copy.wait()
    restrict(now, 0, rows, start_coarse, 0, 2)
    restrict(now, HALO + PLANES, rows, start_coarse, COARSE + 2, 2)
    for t in range(3):
        source, target = fine.at[t % 2], fine.at[(t + 1) % 2]
        fine_planes(source, target, t + 1, HALO)
        fine_planes(source, target, PADDED - 1 - HALO - t, HALO)
    fine_planes(fine.at[1], fine.at[0], HALO, PLANES)
    restrict(now, HALO, rows, end_coarse, 0, COARSE)
    finish = end_coarse[...]
    correction = finish - march(start_coarse[...])
    slots[n, pl.ds(6, 4)] = jnp.where(n == 0, finish, correction)

    term_copy = remote(
        slots.at[n, pl.ds(6, 4)],
        slots.at[n, pl.ds(6, 4)],
        term_send.at[0],
        term_recv.at[n],
        {"cuts": seat(s)},
    )

    def wing_copy(m, source, target, width, step, side, send):
        return remote(
            slots.at[m, pl.ds(6 + source, width)],
            slots.at[m, pl.ds(target, width)],
            send,
            wing_recv.at[m, side],
            {"cuts": seat(at(step)), "space": at(step)},
        )

    wings = (
        ((0, 2, 4, 1, 0), (0, 10, 4, -1, 1), (2, 0, 2, 2, 2), (0, 14, 2, -2, 3)),
        ((0, 2, 4, 1, 0), (0, 10, 4, -1, 1)),
        ((2, 4, 2, 1, 0), (0, 10, 2, -1, 1)),
    )

    def first_wings(m):
        return [wing_copy(m, *wing, first_send.at[wing[4]]) for wing in wings[m]]

    def later_wings(m, kind):
        return [wing_copy(m, *wing, wing_send.at[m, wing[4]]) for wing in wings[kind]]

    for m in range(3):

        @pl.when(n == m)
        def _():
            for copy in first_wings(m):
                copy.start()

    @pl.when(jnp.logical_not(chain))
    def _():
        term_copy.start()

    def await_term(m):
        @pl.when(n != m)
        def _():
            own = slots.at[m, pl.ds(6, 4)]
            remote(own, own, term_send.at[0], term_recv.at[m], {"space": at(1)}).wait_recv()

    def result_copy(m):
        return remote(
            results.at[m], mine, result_send.at[m], result_recv.at[0], {"cuts": m}
        )

    def deliver(m, state):
        results[m] = state

        @pl.when(m != n)
        def _():
            result_copy(m).start()

    def wide_copies(r):
        return [
            remote(
                wides.at[r, pl.ds(8, 4)],
                wides.at[r, pl.ds(target, 4)],
                wide_send.at[r, side],
                wide_recv.at[r, side],
                {"cuts": seat(at(step)), "space": at(step)},
            )
            for target, step, side in ((4, 1, 0), (12, -1, 1), (0, 2, 2), (16, -2, 3))
        ]

    def forward(base):
        for kind in range(3):
            await_term(base + kind)
            for copy in later_wings(base + kind, kind):
                copy.start()

    def three_links(base, wide, r, arrive):
        wide = march(wide)
        arrive(1)
        wide = wide + slots[base + 1, 2:14]
        deliver(base + 1, wide[4:8])
        wide = march(wide)
        arrive(2)
        wide = wide + slots[base + 2, 4:12]
        deliver(base + 2, wide[2:6])
        wide = march(wide)
        await_term(base + 3)
        state = wide + slots[base + 3, 6:10]
        wides[r + 1, pl.ds(8, 4)] = state

        @pl.when(r < rounds - 1)
        def _():
            for copy in wide_copies(r + 1):
                copy.start()
            forward(base + 4)

        deliver(base + 3, state)

    @pl.when(chain)
    def _():
        def arrive_first(m):
            await_term(m)
            for copy in first_wings(m):
                copy.wait_recv()

        arrive_first(0)
        three_links(0, slots[0], 0, arrive_first)

        def one_round(r, carry):
            base = 4 * r

            def arrive(kind):
                for copy in later_wings(base + kind, kind):
                    copy.wait()

            for copy in wide_copies(r):
                copy.wait()
            wide = march(wides[r])
            arrive(0)
            wide = wide + slots[base]
            deliver(base, wide[6:10])
            three_links(base, wide, r, arrive)
            return carry

        lax.fori_loop(1, rounds, one_round, 0)
        for m in range(1, cuts):

            @pl.when(m != n)
            def _():
                result_copy(m).wait_send()

    @pl.when(n == 0)
    def _():
        mine[...] = end_coarse[...]

    @pl.when(chain & (n > 0))
    def _():
        mine[...] = results[n]

    @pl.when(jnp.logical_not(chain) & (n > 0))
    def _():
        result_copy(n).wait_recv()

    change = mine[...] - end_coarse[...]
    even = even_lanes(change.shape)
    for k, (out, spread) in enumerate(
        (
            (out_u, jnp.where(even, change, pltpu.roll(change, 1, 2))),
            (out_v, jnp.where(even, pltpu.roll(change, GZ - 1, 2), change)),
        )
    ):
        for i in range(COARSE):
            slot = k * COARSE + i
            rows[slot, pl.ds(0, CY, stride=2)] = spread[i]
            rows[slot, pl.ds(1, CY, stride=2)] = spread[i]
            added = rows[slot]
            out[0, 2 * i] = fine[0, k, HALO + 2 * i] + added
            out[0, 2 * i + 1] = fine[0, k, HALO + 2 * i + 1] + added

    for m in range(3):

        @pl.when(n == m)
        def _():
            for copy in first_wings(m):
                copy.wait_send()

    @pl.when(jnp.logical_not(chain))
    def _():
        term_copy.wait_send()


def on_device(start_u, start_v):
    cuts = lax.axis_size("cuts")
    space = lax.axis_size("space")
    rounds = cuts // 4
    block = (COARSE, CY, GZ)
    f32 = jnp.float32
    shape = jax.ShapeDtypeStruct((1, PLANES, GY, GZ), f32)
    hbm = pl.BlockSpec(memory_space=pl.ANY)
    vmem = pl.BlockSpec(memory_space=pltpu.VMEM)
    dma = pltpu.SemaphoreType.DMA

    def body(*refs):
        kernel(cuts, space, *refs)

    return pl.pallas_call(
        body,
        out_shape=(shape, shape),
        in_specs=[hbm, hbm],
        out_specs=(vmem, vmem),
        scratch_shapes=[
            pltpu.VMEM((2, 2, PADDED, GY, GZ), f32),
            pltpu.VMEM((PADDED // 2, GY, GZ), f32),
            pltpu.VMEM((PADDED // 2, CY, GZ), f32),
            pltpu.VMEM(block, f32),
            pltpu.VMEM(block, f32),
            pltpu.VMEM((cuts, 16, CY, GZ), f32),
            pltpu.VMEM((rounds + 1, 20, CY, GZ), f32),
            pltpu.VMEM((cuts, *block), f32),
            dma((2,)),
            dma((4,)),
            dma((4,)),
            dma((1,)),
            dma((cuts,)),
            dma((4,)),
            dma((cuts, 4)),
            dma((cuts, 4)),
            dma((rounds, 4)),
            dma((rounds, 4)),
            dma((cuts,)),
            dma((1,)),
        ],
        compiler_params=pltpu.CompilerParams(collective_id=0, has_side_effects=True),
        name="parareal",
    )(start_u, start_v)


def solution(mesh):
    return jax.shard_map(
        on_device,
        mesh=mesh,
        in_specs=(P("cuts", "space", None, None), P("cuts", "space", None, None)),
        out_specs=(P("cuts", "space", None, None), P("cuts", "space", None, None)),
        check_vma=False,
    )
```

```python
import jax
import jax.numpy as jnp
from jax import lax
from jax.experimental import pallas as pl
from jax.experimental.pallas import tpu as pltpu
from jax.sharding import PartitionSpec as P

MESH = pl.DeviceIdType.MESH
GY = 32
GZ = 128
CY = GY // 2
PLANES = 8
COARSE = PLANES // 2
HALO = 4
PADDED = PLANES + 2 * HALO

SPREAD_FIRST = 0.14
SPREAD_SECOND = 0.13
FEED_RATE = 0.035
KILL_RATE = 0.065


def even_lanes(shape):
    return lax.broadcasted_iota(jnp.int32, shape, len(shape) - 1) % 2 == 0


def coarse_step(x):
    inner = x[1:-1]
    even = even_lanes(inner.shape)
    beside = x[2:] + x[:-2]
    beside = beside + pltpu.roll(inner, 1, 1) + pltpu.roll(inner, CY - 1, 1)
    beside = beside + pltpu.roll(inner, 2, 2) + pltpu.roll(inner, GZ - 2, 2)
    other = jnp.where(even, pltpu.roll(inner, GZ - 1, 2), pltpu.roll(inner, 1, 2))
    second = jnp.where(even, other, inner)
    feeding = inner * other * second
    spread = jnp.where(even, 0.5 * SPREAD_FIRST, 0.5 * SPREAD_SECOND)
    keep = jnp.where(
        even,
        1.0 - 3.0 * SPREAD_FIRST - 2.0 * FEED_RATE,
        1.0 - 3.0 * SPREAD_SECOND - 2.0 * (FEED_RATE + KILL_RATE),
    )
    gain = jnp.where(even, 2.0 * FEED_RATE, 0.0)
    sign = jnp.where(even, -2.0, 2.0)
    return keep * inner + spread * beside + gain + sign * feeding


def march(x):
    return coarse_step(coarse_step(x))


def fine_planes(source, target, first, count):
    def body(step, carry):
        p = first + step
        u = source[0, p]
        v = source[1, p]
        feeding = u * v * v
        beside = source[0, p - 1] + source[0, p + 1]
        beside = beside + pltpu.roll(u, 1, 0) + pltpu.roll(u, GY - 1, 0)
        beside = beside + pltpu.roll(u, 1, 1) + pltpu.roll(u, GZ - 1, 1)
        target[0, p] = (
            (1.0 - 6.0 * SPREAD_FIRST - FEED_RATE) * u + SPREAD_FIRST * beside + FEED_RATE - feeding
        )
        beside = source[1, p - 1] + source[1, p + 1]
        beside = beside + pltpu.roll(v, 1, 0) + pltpu.roll(v, GY - 1, 0)
        beside = beside + pltpu.roll(v, 1, 1) + pltpu.roll(v, GZ - 1, 1)
        target[1, p] = (
            (1.0 - 6.0 * SPREAD_SECOND - FEED_RATE - KILL_RATE) * v
            + SPREAD_SECOND * beside
            + feeding
        )
        return carry

    lax.fori_loop(0, count, body, 0, unroll=2)


def restrict(source, first, rows, out, place, count):
    def body(i, carry):
        p = first + 2 * i
        u = source[0, p] + source[0, p + 1]
        v = source[1, p] + source[1, p + 1]
        even = even_lanes(u.shape)
        rows[i] = jnp.where(even, u + pltpu.roll(u, GZ - 1, 1), v + pltpu.roll(v, 1, 1))
        out[place + i] = 0.125 * (
            rows[i, pl.ds(0, CY, stride=2)] + rows[i, pl.ds(1, CY, stride=2)]
        )
        return carry

    lax.fori_loop(0, count, body, 0)


def kernel(
    cuts,
    space,
    u_ref,
    v_ref,
    finals,
    change_ref,
    fine,
    rows,
    start_coarse,
    end_coarse,
    mine,
    slots,
    wides,
    results,
    load_sem,
    fine_send,
    fine_recv,
    turn,
    term_send,
    term_recv,
    first_send,
    wing_send,
    wing_recv,
    wide_send,
    wide_recv,
    result_send,
    result_recv,
):
    n = lax.axis_index("cuts")
    s = lax.axis_index("space")
    rounds = cuts // 4
    half = cuts // 2
    upper = n >= half
    row = lax.rem(s, 8)
    edge = (row == 7, row == 0)

    def at(step):
        return lax.rem(s + step + space, space)

    def seat(place):
        return lax.rem(place, 8) // 4 * 8

    chain = n == seat(s)
    barrier = pltpu.get_barrier_semaphore()

    def greet(device):
        pl.semaphore_signal(barrier, inc=1, device_id=device, device_id_type=MESH)

    def remote(source, target, send, recv, device):
        return pltpu.make_async_remote_copy(
            src_ref=source,
            dst_ref=target,
            send_sem=send,
            recv_sem=recv,
            device_id=device,
            device_id_type=MESH,
        )

    greet({"space": at(-1)})
    greet({"space": at(1)})
    @pl.when(chain)
    def _():
        for d in range(1, cuts):
            greet({"cuts": lax.rem(n + d, cuts)})
        for step in (-2, -1, 1, 2):
            greet({"cuts": seat(at(step)), "space": at(step)})
            greet({"cuts": 0, "space": at(step)})
        for m in (1, 2):
            for step in (-1, 1):
                greet({"cuts": m, "space": at(step)})

    @pl.when(jnp.logical_not(chain))
    def _():
        greet({"cuts": seat(s)})

    @pl.when(upper & (edge[0] | edge[1]))
    def _():
        greet({"cuts": n - half})

    now = fine.at[0]
    loads = []
    for k, ref in enumerate((u_ref, v_ref)):
        loads.append(
            pltpu.make_async_copy(ref.at[0], now.at[k, pl.ds(HALO, PLANES)], load_sem.at[k])
        )
    for load in loads:
        load.start()

    targets = 2 + jnp.where(chain, 4 + cuts - 1, 1)
    targets = targets + jnp.where(jnp.logical_not(upper) & (edge[0] | edge[1]), 1, 0)
    targets = targets + jnp.where(n == 0, 4, 0) + jnp.where((n == 1) | (n == 2), 2, 0)
    pl.semaphore_wait(barrier, targets)

    copies = []
    for k, ref in enumerate((u_ref, v_ref)):
        copies.append(
            remote(
                ref.at[0, pl.ds(PLANES - HALO, HALO)],
                now.at[k, pl.ds(0, HALO)],
                fine_send.at[2 * k],
                fine_recv.at[2 * k],
                {"space": at(1)},
            )
        )
        copies.append(
            remote(
                ref.at[0, pl.ds(0, HALO)],
                now.at[k, pl.ds(HALO + PLANES, HALO)],
                fine_send.at[2 * k + 1],
                fine_recv.at[2 * k + 1],
                {"space": at(-1)},
            )
        )
    def start(which):
        for copy in copies[which::2]:
            copy.start()

    for which in range(2):

        @pl.when(jnp.logical_not(upper & edge[which]))
        def _():
            start(which)

    for load in loads:
        load.wait()

    restrict(now, HALO, rows, start_coarse, 2, COARSE)
    for t in range(3):
        fine_planes(fine.at[t % 2], fine.at[(t + 1) % 2], HALO + 1 + t, PLANES - 2 - 2 * t)
    for which in range(2):

        @pl.when(upper & edge[which])
        def _():
            pl.semaphore_wait(turn, 1)
            start(which)

        @pl.when(jnp.logical_not(upper) & edge[which])
        def _():
            for copy in copies[which::2]:
                copy.wait_send()
            pl.semaphore_signal(
                turn, inc=1, device_id={"cuts": n + half}, device_id_type=MESH
            )

    for copy in copies:
        copy.wait_recv()
    restrict(now, 0, rows, start_coarse, 0, 2)
    restrict(now, HALO + PLANES, rows, start_coarse, COARSE + 2, 2)
    for t in range(3):
        source, target = fine.at[t % 2], fine.at[(t + 1) % 2]
        fine_planes(source, target, t + 1, HALO)
        fine_planes(source, target, PADDED - 1 - HALO - t, HALO)
    fine_planes(fine.at[1], fine.at[0], HALO, PLANES)
    outs = [
        pltpu.make_async_copy(now.at[k, pl.ds(HALO, PLANES)], finals.at[k], load_sem.at[k])
        for k in range(2)
    ]
    restrict(now, HALO, rows, end_coarse, 0, COARSE)
    finish = end_coarse[...]
    correction = finish - march(start_coarse[...])
    slots[n, pl.ds(6, 4)] = jnp.where(n == 0, finish, correction)

    term_copy = remote(
        slots.at[n, pl.ds(6, 4)],
        slots.at[n, pl.ds(6, 4)],
        term_send.at[0],
        term_recv.at[n],
        {"cuts": seat(s)},
    )

    def wing_copy(m, source, target, width, step, side, send):
        return remote(
            slots.at[m, pl.ds(6 + source, width)],
            slots.at[m, pl.ds(target, width)],
            send,
            wing_recv.at[m, side],
            {"cuts": seat(at(step)), "space": at(step)},
        )

    wings = (
        ((0, 2, 4, 1, 0), (0, 10, 4, -1, 1), (2, 0, 2, 2, 2), (0, 14, 2, -2, 3)),
        ((0, 2, 4, 1, 0), (0, 10, 4, -1, 1)),
        ((2, 4, 2, 1, 0), (0, 10, 2, -1, 1)),
    )

    def first_wings(m):
        return [wing_copy(m, *wing, first_send.at[wing[4]]) for wing in wings[m]]

    def later_wings(m, kind):
        return [wing_copy(m, *wing, wing_send.at[m, wing[4]]) for wing in wings[kind]]

    for m in range(3):

        @pl.when(n == m)
        def _():
            for copy in first_wings(m):
                copy.start()

    @pl.when(jnp.logical_not(chain))
    def _():
        term_copy.start()

    for out in outs:
        out.start()

    def await_term(m):
        @pl.when(n != m)
        def _():
            own = slots.at[m, pl.ds(6, 4)]
            remote(own, own, term_send.at[0], term_recv.at[m], {"space": at(1)}).wait_recv()

    def result_copy(m):
        return remote(
            results.at[m], mine, result_send.at[m], result_recv.at[0], {"cuts": m}
        )

    def deliver(m, state):
        results[m] = state

        @pl.when(m != n)
        def _():
            result_copy(m).start()

    def wide_copies(r):
        return [
            remote(
                wides.at[r, pl.ds(8, 4)],
                wides.at[r, pl.ds(target, 4)],
                wide_send.at[r, side],
                wide_recv.at[r, side],
                {"cuts": seat(at(step)), "space": at(step)},
            )
            for target, step, side in ((4, 1, 0), (12, -1, 1), (0, 2, 2), (16, -2, 3))
        ]

    def forward(base):
        for kind in range(3):
            await_term(base + kind)
            for copy in later_wings(base + kind, kind):
                copy.start()

    def three_links(base, wide, r, arrive):
        wide = march(wide)
        arrive(1)
        wide = wide + slots[base + 1, 2:14]
        deliver(base + 1, wide[4:8])
        wide = march(wide)
        arrive(2)
        wide = wide + slots[base + 2, 4:12]
        deliver(base + 2, wide[2:6])
        wide = march(wide)
        await_term(base + 3)
        state = wide + slots[base + 3, 6:10]
        wides[r + 1, pl.ds(8, 4)] = state

        @pl.when(r < rounds - 1)
        def _():
            for copy in wide_copies(r + 1):
                copy.start()
            forward(base + 4)

        deliver(base + 3, state)

    @pl.when(chain)
    def _():
        def arrive_first(m):
            await_term(m)
            for copy in first_wings(m):
                copy.wait_recv()

        arrive_first(0)
        three_links(0, slots[0], 0, arrive_first)

        def one_round(r, carry):
            base = 4 * r

            def arrive(kind):
                for copy in later_wings(base + kind, kind):
                    copy.wait()

            for copy in wide_copies(r):
                copy.wait()
            wide = march(wides[r])
            arrive(0)
            wide = wide + slots[base]
            deliver(base, wide[6:10])
            three_links(base, wide, r, arrive)
            return carry

        lax.fori_loop(1, rounds, one_round, 0)
        for m in range(1, cuts):

            @pl.when(m != n)
            def _():
                result_copy(m).wait_send()

    @pl.when(n == 0)
    def _():
        mine[...] = end_coarse[...]

    @pl.when(chain & (n > 0))
    def _():
        mine[...] = results[n]

    @pl.when(jnp.logical_not(chain) & (n > 0))
    def _():
        result_copy(n).wait_recv()

    change_ref[...] = mine[...] - end_coarse[...]
    for out in outs:
        out.wait()

    for m in range(3):

        @pl.when(n == m)
        def _():
            for copy in first_wings(m):
                copy.wait_send()

    @pl.when(jnp.logical_not(chain))
    def _():
        term_copy.wait_send()

    for which in range(2):

        @pl.when(upper | jnp.logical_not(edge[which]))
        def _():
            for copy in copies[which::2]:
                copy.wait_send()


def finish_kernel(finals, change_ref, out_u, out_v, rows):
    change = change_ref[...]
    even = even_lanes(change.shape)
    for k, (out, spread) in enumerate(
        (
            (out_u, jnp.where(even, change, pltpu.roll(change, 1, 2))),
            (out_v, jnp.where(even, pltpu.roll(change, GZ - 1, 2), change)),
        )
    ):
        for i in range(COARSE):
            slot = k * COARSE + i
            rows[slot, pl.ds(0, CY, stride=2)] = spread[i]
            rows[slot, pl.ds(1, CY, stride=2)] = spread[i]
            added = rows[slot]
            out[0, 2 * i] = finals[k, 2 * i] + added
            out[0, 2 * i + 1] = finals[k, 2 * i + 1] + added


def on_device(start_u, start_v):
    cuts = lax.axis_size("cuts")
    space = lax.axis_size("space")
    rounds = cuts // 4
    block = (COARSE, CY, GZ)
    f32 = jnp.float32
    shape = jax.ShapeDtypeStruct((1, PLANES, GY, GZ), f32)
    hbm = pl.BlockSpec(memory_space=pl.ANY)
    vmem = pl.BlockSpec(memory_space=pltpu.VMEM)
    dma = pltpu.SemaphoreType.DMA

    def body(*refs):
        kernel(cuts, space, *refs)

    finals, change = pl.pallas_call(
        body,
        out_shape=(
            jax.ShapeDtypeStruct((2, PLANES, GY, GZ), f32),
            jax.ShapeDtypeStruct(block, f32),
        ),
        in_specs=[hbm, hbm],
        out_specs=(hbm, vmem),
        scratch_shapes=[
            pltpu.VMEM((2, 2, PADDED, GY, GZ), f32),
            pltpu.VMEM((PADDED // 2, GY, GZ), f32),
            pltpu.VMEM((PADDED // 2, CY, GZ), f32),
            pltpu.VMEM(block, f32),
            pltpu.VMEM(block, f32),
            pltpu.VMEM((cuts, 16, CY, GZ), f32),
            pltpu.VMEM((rounds + 1, 20, CY, GZ), f32),
            pltpu.VMEM((cuts, *block), f32),
            dma((2,)),
            dma((4,)),
            dma((4,)),
            pltpu.SemaphoreType.REGULAR,
            dma((1,)),
            dma((cuts,)),
            dma((4,)),
            dma((cuts, 4)),
            dma((cuts, 4)),
            dma((rounds, 4)),
            dma((rounds, 4)),
            dma((cuts,)),
            dma((1,)),
        ],
        compiler_params=pltpu.CompilerParams(collective_id=0, has_side_effects=True),
        name="parareal",
    )(start_u, start_v)
    return pl.pallas_call(
        finish_kernel,
        out_shape=(shape, shape),
        in_specs=[vmem, vmem],
        out_specs=(vmem, vmem),
        scratch_shapes=[pltpu.VMEM((2 * COARSE, GY, GZ), f32)],
        name="finish",
    )(finals, change)


def solution(mesh):
    return jax.shard_map(
        on_device,
        mesh=mesh,
        in_specs=(P("cuts", "space", None, None), P("cuts", "space", None, None)),
        out_specs=(P("cuts", "space", None, None), P("cuts", "space", None, None)),
        check_vma=False,
    )
```

```python
import jax
import jax.numpy as jnp
from jax import lax
from jax.experimental import pallas as pl
from jax.experimental.pallas import tpu as pltpu
from jax.sharding import PartitionSpec as P

MESH = pl.DeviceIdType.MESH
GY = 32
GZ = 128
CY = GY // 2
PLANES = 8
COARSE = PLANES // 2
HALO = 4
PADDED = PLANES + 2 * HALO

SPREAD_FIRST = 0.14
SPREAD_SECOND = 0.13
FEED_RATE = 0.035
KILL_RATE = 0.065


def even_lanes(shape):
    return lax.broadcasted_iota(jnp.int32, shape, len(shape) - 1) % 2 == 0


def coarse_step(x):
    inner = x[1:-1]
    even = even_lanes(inner.shape)
    beside = x[2:] + x[:-2]
    beside = beside + pltpu.roll(inner, 1, 1) + pltpu.roll(inner, CY - 1, 1)
    beside = beside + pltpu.roll(inner, 2, 2) + pltpu.roll(inner, GZ - 2, 2)
    other = jnp.where(even, pltpu.roll(inner, GZ - 1, 2), pltpu.roll(inner, 1, 2))
    second = jnp.where(even, other, inner)
    feeding = inner * other * second
    spread = jnp.where(even, 0.5 * SPREAD_FIRST, 0.5 * SPREAD_SECOND)
    keep = jnp.where(
        even,
        1.0 - 3.0 * SPREAD_FIRST - 2.0 * FEED_RATE,
        1.0 - 3.0 * SPREAD_SECOND - 2.0 * (FEED_RATE + KILL_RATE),
    )
    gain = jnp.where(even, 2.0 * FEED_RATE, 0.0)
    sign = jnp.where(even, -2.0, 2.0)
    return keep * inner + spread * beside + gain + sign * feeding


def march(x):
    return coarse_step(coarse_step(x))


def fine_planes(source, target, first, count):
    def body(step, carry):
        p = first + step
        u = source[0, p]
        v = source[1, p]
        feeding = u * v * v
        beside = source[0, p - 1] + source[0, p + 1]
        beside = beside + pltpu.roll(u, 1, 0) + pltpu.roll(u, GY - 1, 0)
        beside = beside + pltpu.roll(u, 1, 1) + pltpu.roll(u, GZ - 1, 1)
        target[0, p] = (
            (1.0 - 6.0 * SPREAD_FIRST - FEED_RATE) * u + SPREAD_FIRST * beside + FEED_RATE - feeding
        )
        beside = source[1, p - 1] + source[1, p + 1]
        beside = beside + pltpu.roll(v, 1, 0) + pltpu.roll(v, GY - 1, 0)
        beside = beside + pltpu.roll(v, 1, 1) + pltpu.roll(v, GZ - 1, 1)
        target[1, p] = (
            (1.0 - 6.0 * SPREAD_SECOND - FEED_RATE - KILL_RATE) * v
            + SPREAD_SECOND * beside
            + feeding
        )
        return carry

    lax.fori_loop(0, count, body, 0, unroll=2)


def restrict(source, first, rows, out, place, count):
    def body(i, carry):
        p = first + 2 * i
        u = source[0, p] + source[0, p + 1]
        v = source[1, p] + source[1, p + 1]
        even = even_lanes(u.shape)
        rows[i] = jnp.where(even, u + pltpu.roll(u, GZ - 1, 1), v + pltpu.roll(v, 1, 1))
        out[place + i] = 0.125 * (
            rows[i, pl.ds(0, CY, stride=2)] + rows[i, pl.ds(1, CY, stride=2)]
        )
        return carry

    lax.fori_loop(0, count, body, 0)


def kernel(
    cuts,
    space,
    u_ref,
    v_ref,
    finals,
    change_ref,
    fine,
    rows,
    start_coarse,
    end_coarse,
    mine,
    slots,
    wides,
    results,
    load_sem,
    fine_send,
    fine_recv,
    turn,
    term_send,
    term_recv,
    first_send,
    wing_send,
    wing_recv,
    wide_send,
    wide_recv,
    result_send,
    result_recv,
):
    n = lax.axis_index("cuts")
    s = lax.axis_index("space")
    rounds = cuts // 4
    half = cuts // 2
    upper = n >= half
    row = lax.rem(s, 8)
    edge = (row == 7, row == 0)

    def at(step):
        return lax.rem(s + step + space, space)

    def seat(place):
        return lax.rem(place, 8) // 4 * 8

    chain = n == seat(s)
    barrier = pltpu.get_barrier_semaphore()

    def greet(device):
        pl.semaphore_signal(barrier, inc=1, device_id=device, device_id_type=MESH)

    def remote(source, target, send, recv, device):
        return pltpu.make_async_remote_copy(
            src_ref=source,
            dst_ref=target,
            send_sem=send,
            recv_sem=recv,
            device_id=device,
            device_id_type=MESH,
        )

    greet({"space": at(-1)})
    greet({"space": at(1)})
    @pl.when(chain)
    def _():
        for d in range(1, cuts):
            greet({"cuts": lax.rem(n + d, cuts)})
        for step in (-2, -1, 1, 2):
            greet({"cuts": seat(at(step)), "space": at(step)})
            greet({"cuts": 0, "space": at(step)})
        for m in (1, 2):
            for step in (-1, 1):
                greet({"cuts": m, "space": at(step)})

    @pl.when(jnp.logical_not(chain))
    def _():
        greet({"cuts": seat(s)})

    @pl.when(upper & (edge[0] | edge[1]))
    def _():
        greet({"cuts": n - half})

    now = fine.at[0]
    loads = []
    for k, ref in enumerate((u_ref, v_ref)):
        loads.append(
            pltpu.make_async_copy(ref.at[0], now.at[k, pl.ds(HALO, PLANES)], load_sem.at[k])
        )
    for load in loads:
        load.start()

    targets = 2 + jnp.where(chain, 4 + cuts - 1, 1)
    targets = targets + jnp.where(jnp.logical_not(upper) & (edge[0] | edge[1]), 1, 0)
    targets = targets + jnp.where(n == 0, 4, 0) + jnp.where((n == 1) | (n == 2), 2, 0)
    pl.semaphore_wait(barrier, targets)

    copies = []
    for k, ref in enumerate((u_ref, v_ref)):
        copies.append(
            remote(
                ref.at[0, pl.ds(PLANES - HALO, HALO)],
                now.at[k, pl.ds(0, HALO)],
                fine_send.at[2 * k],
                fine_recv.at[2 * k],
                {"space": at(1)},
            )
        )
        copies.append(
            remote(
                ref.at[0, pl.ds(0, HALO)],
                now.at[k, pl.ds(HALO + PLANES, HALO)],
                fine_send.at[2 * k + 1],
                fine_recv.at[2 * k + 1],
                {"space": at(-1)},
            )
        )
    def start(which):
        for copy in copies[which::2]:
            copy.start()

    for which in range(2):

        @pl.when(jnp.logical_not(upper & edge[which]))
        def _():
            start(which)

    for load in loads:
        load.wait()

    restrict(now, HALO, rows, start_coarse, 2, COARSE)
    for t in range(3):
        fine_planes(fine.at[t % 2], fine.at[(t + 1) % 2], HALO + 1 + t, PLANES - 2 - 2 * t)
    for which in range(2):

        @pl.when(upper & edge[which])
        def _():
            pl.semaphore_wait(turn, 1)
            start(which)

        @pl.when(jnp.logical_not(upper) & edge[which])
        def _():
            for copy in copies[which::2]:
                copy.wait_send()
            pl.semaphore_signal(
                turn, inc=1, device_id={"cuts": n + half}, device_id_type=MESH
            )

    for copy in copies:
        copy.wait_recv()
    restrict(now, 0, rows, start_coarse, 0, 2)
    restrict(now, HALO + PLANES, rows, start_coarse, COARSE + 2, 2)
    for t in range(3):
        source, target = fine.at[t % 2], fine.at[(t + 1) % 2]
        fine_planes(source, target, t + 1, HALO)
        fine_planes(source, target, PADDED - 1 - HALO - t, HALO)
    fine_planes(fine.at[1], fine.at[0], HALO, PLANES)
    outs = [
        pltpu.make_async_copy(now.at[k, pl.ds(HALO, PLANES)], finals.at[k], load_sem.at[k])
        for k in range(2)
    ]
    restrict(now, HALO, rows, end_coarse, 0, COARSE)
    finish = end_coarse[...]
    correction = finish - march(start_coarse[...])
    slots[n, pl.ds(6, 4)] = jnp.where(n == 0, finish, correction)

    term_copy = remote(
        slots.at[n, pl.ds(6, 4)],
        slots.at[n, pl.ds(6, 4)],
        term_send.at[0],
        term_recv.at[n],
        {"cuts": seat(s)},
    )

    def wing_copy(m, source, target, width, step, side, send):
        return remote(
            slots.at[m, pl.ds(6 + source, width)],
            slots.at[m, pl.ds(target, width)],
            send,
            wing_recv.at[m, side],
            {"cuts": seat(at(step)), "space": at(step)},
        )

    wings = (
        ((2, 0, 2, 2, 2), (0, 14, 2, -2, 3), (0, 2, 4, 1, 0), (0, 10, 4, -1, 1)),
        ((0, 2, 4, 1, 0), (0, 10, 4, -1, 1)),
        ((2, 4, 2, 1, 0), (0, 10, 2, -1, 1)),
    )

    def first_wings(m):
        return [wing_copy(m, *wing, first_send.at[wing[4]]) for wing in wings[m]]

    def later_wings(m, kind):
        return [wing_copy(m, *wing, wing_send.at[m, wing[4]]) for wing in wings[kind]]

    for m in range(3):

        @pl.when(n == m)
        def _():
            for copy in first_wings(m):
                copy.start()

    @pl.when(jnp.logical_not(chain))
    def _():
        term_copy.start()

    for out in outs:
        out.start()

    def await_term(m):
        @pl.when(n != m)
        def _():
            own = slots.at[m, pl.ds(6, 4)]
            remote(own, own, term_send.at[0], term_recv.at[m], {"space": at(1)}).wait_recv()

    def result_copy(m):
        return remote(
            results.at[m], mine, result_send.at[m], result_recv.at[0], {"cuts": m}
        )

    def deliver(m, state):
        results[m] = state

        @pl.when(m != n)
        def _():
            result_copy(m).start()

    def wide_copies(r):
        return [
            remote(
                wides.at[r, pl.ds(8, 4)],
                wides.at[r, pl.ds(target, 4)],
                wide_send.at[r, side],
                wide_recv.at[r, side],
                {"cuts": seat(at(step)), "space": at(step)},
            )
            for target, step, side in ((0, 2, 2), (16, -2, 3), (4, 1, 0), (12, -1, 1))
        ]

    def forward(base):
        for kind in range(3):
            await_term(base + kind)
            for copy in later_wings(base + kind, kind):
                copy.start()

    def three_links(base, wide, r, arrive):
        wide = march(wide)
        arrive(1)
        wide = wide + slots[base + 1, 2:14]
        deliver(base + 1, wide[4:8])
        wide = march(wide)
        arrive(2)
        wide = wide + slots[base + 2, 4:12]
        deliver(base + 2, wide[2:6])
        wide = march(wide)
        await_term(base + 3)
        state = wide + slots[base + 3, 6:10]
        wides[r + 1, pl.ds(8, 4)] = state

        @pl.when(r < rounds - 1)
        def _():
            for copy in wide_copies(r + 1):
                copy.start()
            forward(base + 4)

        deliver(base + 3, state)

    @pl.when(chain)
    def _():
        def arrive_first(m):
            await_term(m)
            for copy in first_wings(m):
                copy.wait_recv()

        arrive_first(0)
        three_links(0, slots[0], 0, arrive_first)

        def one_round(r, carry):
            base = 4 * r

            def arrive(kind):
                for copy in later_wings(base + kind, kind):
                    copy.wait()

            for copy in wide_copies(r):
                copy.wait()
            wide = march(wides[r])
            arrive(0)
            wide = wide + slots[base]
            deliver(base, wide[6:10])
            three_links(base, wide, r, arrive)
            return carry

        lax.fori_loop(1, rounds, one_round, 0)
        for m in range(1, cuts):

            @pl.when(m != n)
            def _():
                result_copy(m).wait_send()

    @pl.when(n == 0)
    def _():
        mine[...] = end_coarse[...]

    @pl.when(chain & (n > 0))
    def _():
        mine[...] = results[n]

    @pl.when(jnp.logical_not(chain) & (n > 0))
    def _():
        result_copy(n).wait_recv()

    change_ref[...] = mine[...] - end_coarse[...]
    for out in outs:
        out.wait()

    for m in range(3):

        @pl.when(n == m)
        def _():
            for copy in first_wings(m):
                copy.wait_send()

    @pl.when(jnp.logical_not(chain))
    def _():
        term_copy.wait_send()

    for which in range(2):

        @pl.when(upper | jnp.logical_not(edge[which]))
        def _():
            for copy in copies[which::2]:
                copy.wait_send()


def finish_kernel(finals, change_ref, out_u, out_v, rows):
    change = change_ref[...]
    even = even_lanes(change.shape)
    for k, (out, spread) in enumerate(
        (
            (out_u, jnp.where(even, change, pltpu.roll(change, 1, 2))),
            (out_v, jnp.where(even, pltpu.roll(change, GZ - 1, 2), change)),
        )
    ):
        for i in range(COARSE):
            slot = k * COARSE + i
            rows[slot, pl.ds(0, CY, stride=2)] = spread[i]
            rows[slot, pl.ds(1, CY, stride=2)] = spread[i]
            added = rows[slot]
            out[0, 2 * i] = finals[k, 2 * i] + added
            out[0, 2 * i + 1] = finals[k, 2 * i + 1] + added


def on_device(start_u, start_v):
    cuts = lax.axis_size("cuts")
    space = lax.axis_size("space")
    rounds = cuts // 4
    block = (COARSE, CY, GZ)
    f32 = jnp.float32
    shape = jax.ShapeDtypeStruct((1, PLANES, GY, GZ), f32)
    hbm = pl.BlockSpec(memory_space=pl.ANY)
    vmem = pl.BlockSpec(memory_space=pltpu.VMEM)
    dma = pltpu.SemaphoreType.DMA

    def body(*refs):
        kernel(cuts, space, *refs)

    finals, change = pl.pallas_call(
        body,
        out_shape=(
            jax.ShapeDtypeStruct((2, PLANES, GY, GZ), f32),
            jax.ShapeDtypeStruct(block, f32),
        ),
        in_specs=[hbm, hbm],
        out_specs=(hbm, vmem),
        scratch_shapes=[
            pltpu.VMEM((2, 2, PADDED, GY, GZ), f32),
            pltpu.VMEM((PADDED // 2, GY, GZ), f32),
            pltpu.VMEM((PADDED // 2, CY, GZ), f32),
            pltpu.VMEM(block, f32),
            pltpu.VMEM(block, f32),
            pltpu.VMEM((cuts, 16, CY, GZ), f32),
            pltpu.VMEM((rounds + 1, 20, CY, GZ), f32),
            pltpu.VMEM((cuts, *block), f32),
            dma((2,)),
            dma((4,)),
            dma((4,)),
            pltpu.SemaphoreType.REGULAR,
            dma((1,)),
            dma((cuts,)),
            dma((4,)),
            dma((cuts, 4)),
            dma((cuts, 4)),
            dma((rounds, 4)),
            dma((rounds, 4)),
            dma((cuts,)),
            dma((1,)),
        ],
        compiler_params=pltpu.CompilerParams(collective_id=0, has_side_effects=True),
        name="parareal",
    )(start_u, start_v)
    return pl.pallas_call(
        finish_kernel,
        out_shape=(shape, shape),
        in_specs=[vmem, vmem],
        out_specs=(vmem, vmem),
        scratch_shapes=[pltpu.VMEM((2 * COARSE, GY, GZ), f32)],
        name="finish",
    )(finals, change)


def solution(mesh):
    return jax.shard_map(
        on_device,
        mesh=mesh,
        in_specs=(P("cuts", "space", None, None), P("cuts", "space", None, None)),
        out_specs=(P("cuts", "space", None, None), P("cuts", "space", None, None)),
        check_vma=False,
    )
```

```python
import jax
import jax.numpy as jnp
from jax import lax
from jax.experimental import pallas as pl
from jax.experimental.pallas import tpu as pltpu
from jax.sharding import PartitionSpec as P

MESH = pl.DeviceIdType.MESH
GY = 32
GZ = 128
CY = GY // 2
PLANES = 8
COARSE = PLANES // 2
HALO = 4
PADDED = PLANES + 2 * HALO

SPREAD_FIRST = 0.14
SPREAD_SECOND = 0.13
FEED_RATE = 0.035
KILL_RATE = 0.065


def even_lanes(shape):
    return lax.broadcasted_iota(jnp.int32, shape, len(shape) - 1) % 2 == 0


def coarse_step(x):
    inner = x[1:-1]
    even = even_lanes(inner.shape)
    beside = x[2:] + x[:-2]
    beside = beside + pltpu.roll(inner, 1, 1) + pltpu.roll(inner, CY - 1, 1)
    beside = beside + pltpu.roll(inner, 2, 2) + pltpu.roll(inner, GZ - 2, 2)
    other = jnp.where(even, pltpu.roll(inner, GZ - 1, 2), pltpu.roll(inner, 1, 2))
    second = jnp.where(even, other, inner)
    feeding = inner * other * second
    spread = jnp.where(even, 0.5 * SPREAD_FIRST, 0.5 * SPREAD_SECOND)
    keep = jnp.where(
        even,
        1.0 - 3.0 * SPREAD_FIRST - 2.0 * FEED_RATE,
        1.0 - 3.0 * SPREAD_SECOND - 2.0 * (FEED_RATE + KILL_RATE),
    )
    gain = jnp.where(even, 2.0 * FEED_RATE, 0.0)
    sign = jnp.where(even, -2.0, 2.0)
    return keep * inner + spread * beside + gain + sign * feeding


def march(x):
    return coarse_step(coarse_step(x))


def fine_planes(source, target, first, count):
    def body(step, carry):
        p = first + step
        u = source[0, p]
        v = source[1, p]
        feeding = u * v * v
        beside = source[0, p - 1] + source[0, p + 1]
        beside = beside + pltpu.roll(u, 1, 0) + pltpu.roll(u, GY - 1, 0)
        beside = beside + pltpu.roll(u, 1, 1) + pltpu.roll(u, GZ - 1, 1)
        target[0, p] = (
            (1.0 - 6.0 * SPREAD_FIRST - FEED_RATE) * u + SPREAD_FIRST * beside + FEED_RATE - feeding
        )
        beside = source[1, p - 1] + source[1, p + 1]
        beside = beside + pltpu.roll(v, 1, 0) + pltpu.roll(v, GY - 1, 0)
        beside = beside + pltpu.roll(v, 1, 1) + pltpu.roll(v, GZ - 1, 1)
        target[1, p] = (
            (1.0 - 6.0 * SPREAD_SECOND - FEED_RATE - KILL_RATE) * v
            + SPREAD_SECOND * beside
            + feeding
        )
        return carry

    lax.fori_loop(0, count, body, 0, unroll=2 if count % 4 else 4)


def restrict(source, first, rows, out, place, count):
    def body(i, carry):
        p = first + 2 * i
        u = source[0, p] + source[0, p + 1]
        v = source[1, p] + source[1, p + 1]
        even = even_lanes(u.shape)
        rows[i] = jnp.where(even, u + pltpu.roll(u, GZ - 1, 1), v + pltpu.roll(v, 1, 1))
        out[place + i] = 0.125 * (
            rows[i, pl.ds(0, CY, stride=2)] + rows[i, pl.ds(1, CY, stride=2)]
        )
        return carry

    lax.fori_loop(0, count, body, 0, unroll=2)


def kernel(
    cuts,
    space,
    u_ref,
    v_ref,
    finals,
    change_ref,
    fine,
    rows,
    start_coarse,
    end_coarse,
    mine,
    slots,
    wides,
    results,
    load_sem,
    fine_send,
    fine_recv,
    turn,
    term_send,
    term_recv,
    first_send,
    wing_send,
    wing_recv,
    wide_send,
    wide_recv,
    result_send,
    result_recv,
):
    n = lax.axis_index("cuts")
    s = lax.axis_index("space")
    rounds = cuts // 4
    half = cuts // 2
    upper = n >= half
    row = lax.rem(s, 8)
    edge = (row == 7, row == 0)

    def at(step):
        return lax.rem(s + step + space, space)

    def seat(place):
        return lax.rem(place, 8) // 4 * 8

    chain = n == seat(s)
    barrier = pltpu.get_barrier_semaphore()

    def greet(device):
        pl.semaphore_signal(barrier, inc=1, device_id=device, device_id_type=MESH)

    def remote(source, target, send, recv, device):
        return pltpu.make_async_remote_copy(
            src_ref=source,
            dst_ref=target,
            send_sem=send,
            recv_sem=recv,
            device_id=device,
            device_id_type=MESH,
        )

    greet({"space": at(-1)})
    greet({"space": at(1)})
    @pl.when(chain)
    def _():
        for d in range(1, cuts):
            greet({"cuts": lax.rem(n + d, cuts)})
        for step in (-2, -1, 1, 2):
            greet({"cuts": seat(at(step)), "space": at(step)})
            greet({"cuts": 0, "space": at(step)})
        for m in (1, 2):
            for step in (-1, 1):
                greet({"cuts": m, "space": at(step)})

    @pl.when(jnp.logical_not(chain))
    def _():
        greet({"cuts": seat(s)})

    @pl.when(upper & (edge[0] | edge[1]))
    def _():
        greet({"cuts": n - half})

    now = fine.at[0]
    loads = []
    for k, ref in enumerate((u_ref, v_ref)):
        loads.append(
            pltpu.make_async_copy(ref.at[0], now.at[k, pl.ds(HALO, PLANES)], load_sem.at[k])
        )
    for load in loads:
        load.start()

    targets = 2 + jnp.where(chain, 4 + cuts - 1, 1)
    targets = targets + jnp.where(jnp.logical_not(upper) & (edge[0] | edge[1]), 1, 0)
    targets = targets + jnp.where(n == 0, 4, 0) + jnp.where((n == 1) | (n == 2), 2, 0)
    pl.semaphore_wait(barrier, targets)

    copies = []
    for k, ref in enumerate((u_ref, v_ref)):
        copies.append(
            remote(
                ref.at[0, pl.ds(PLANES - HALO, HALO)],
                now.at[k, pl.ds(0, HALO)],
                fine_send.at[2 * k],
                fine_recv.at[2 * k],
                {"space": at(1)},
            )
        )
        copies.append(
            remote(
                ref.at[0, pl.ds(0, HALO)],
                now.at[k, pl.ds(HALO + PLANES, HALO)],
                fine_send.at[2 * k + 1],
                fine_recv.at[2 * k + 1],
                {"space": at(-1)},
            )
        )
    def start(which):
        for copy in copies[which::2]:
            copy.start()

    for which in range(2):

        @pl.when(jnp.logical_not(upper & edge[which]))
        def _():
            start(which)

    for load in loads:
        load.wait()

    restrict(now, HALO, rows, start_coarse, 2, COARSE)
    for t in range(3):
        fine_planes(fine.at[t % 2], fine.at[(t + 1) % 2], HALO + 1 + t, PLANES - 2 - 2 * t)
    for which in range(2):

        @pl.when(upper & edge[which])
        def _():
            pl.semaphore_wait(turn, 1)
            start(which)

        @pl.when(jnp.logical_not(upper) & edge[which])
        def _():
            for copy in copies[which::2]:
                copy.wait_send()
            pl.semaphore_signal(
                turn, inc=1, device_id={"cuts": n + half}, device_id_type=MESH
            )

    for copy in copies:
        copy.wait_recv()
    restrict(now, 0, rows, start_coarse, 0, 2)
    restrict(now, HALO + PLANES, rows, start_coarse, COARSE + 2, 2)
    for t in range(3):
        source, target = fine.at[t % 2], fine.at[(t + 1) % 2]
        fine_planes(source, target, t + 1, HALO)
        fine_planes(source, target, PADDED - 1 - HALO - t, HALO)
    fine_planes(fine.at[1], fine.at[0], HALO, PLANES)
    outs = [
        pltpu.make_async_copy(now.at[k, pl.ds(HALO, PLANES)], finals.at[k], load_sem.at[k])
        for k in range(2)
    ]
    restrict(now, HALO, rows, end_coarse, 0, COARSE)
    finish = end_coarse[...]
    correction = finish - march(start_coarse[...])
    slots[n, pl.ds(6, 4)] = jnp.where(n == 0, finish, correction)

    term_copy = remote(
        slots.at[n, pl.ds(6, 4)],
        slots.at[n, pl.ds(6, 4)],
        term_send.at[0],
        term_recv.at[n],
        {"cuts": seat(s)},
    )

    def wing_copy(m, source, target, width, step, side, send):
        return remote(
            slots.at[m, pl.ds(6 + source, width)],
            slots.at[m, pl.ds(target, width)],
            send,
            wing_recv.at[m, side],
            {"cuts": seat(at(step)), "space": at(step)},
        )

    wings = (
        ((2, 0, 2, 2, 2), (0, 14, 2, -2, 3), (0, 2, 4, 1, 0), (0, 10, 4, -1, 1)),
        ((0, 2, 4, 1, 0), (0, 10, 4, -1, 1)),
        ((2, 4, 2, 1, 0), (0, 10, 2, -1, 1)),
    )

    def first_wings(m):
        return [wing_copy(m, *wing, first_send.at[wing[4]]) for wing in wings[m]]

    def later_wings(m, kind):
        return [wing_copy(m, *wing, wing_send.at[m, wing[4]]) for wing in wings[kind]]

    for m in range(3):

        @pl.when(n == m)
        def _():
            for copy in first_wings(m):
                copy.start()

    @pl.when(jnp.logical_not(chain))
    def _():
        term_copy.start()

    for out in outs:
        out.start()

    def await_term(m):
        @pl.when(n != m)
        def _():
            own = slots.at[m, pl.ds(6, 4)]
            remote(own, own, term_send.at[0], term_recv.at[m], {"space": at(1)}).wait_recv()

    def result_copy(m):
        return remote(
            results.at[m], mine, result_send.at[m], result_recv.at[0], {"cuts": m}
        )

    def deliver(m, state):
        results[m] = state

        @pl.when(m != n)
        def _():
            result_copy(m).start()

    def wide_copies(r):
        return [
            remote(
                wides.at[r, pl.ds(8, 4)],
                wides.at[r, pl.ds(target, 4)],
                wide_send.at[r, side],
                wide_recv.at[r, side],
                {"cuts": seat(at(step)), "space": at(step)},
            )
            for target, step, side in ((0, 2, 2), (16, -2, 3), (4, 1, 0), (12, -1, 1))
        ]

    def forward(base):
        for kind in range(3):
            await_term(base + kind)
            for copy in later_wings(base + kind, kind):
                copy.start()

    def three_links(base, wide, r, arrive):
        wide = march(wide)
        arrive(1)
        wide = wide + slots[base + 1, 2:14]
        deliver(base + 1, wide[4:8])
        wide = march(wide)
        arrive(2)
        wide = wide + slots[base + 2, 4:12]
        deliver(base + 2, wide[2:6])
        wide = march(wide)
        await_term(base + 3)
        state = wide + slots[base + 3, 6:10]
        wides[r + 1, pl.ds(8, 4)] = state

        @pl.when(r < rounds - 1)
        def _():
            for copy in wide_copies(r + 1):
                copy.start()
            forward(base + 4)

        deliver(base + 3, state)

    @pl.when(chain)
    def _():
        def arrive_first(m):
            await_term(m)
            for copy in first_wings(m):
                copy.wait_recv()

        arrive_first(0)
        three_links(0, slots[0], 0, arrive_first)

        def one_round(r, carry):
            base = 4 * r

            def arrive(kind):
                for copy in later_wings(base + kind, kind):
                    copy.wait()

            for copy in wide_copies(r):
                copy.wait()
            wide = march(wides[r])
            arrive(0)
            wide = wide + slots[base]
            deliver(base, wide[6:10])
            three_links(base, wide, r, arrive)
            return carry

        lax.fori_loop(1, rounds, one_round, 0)
        for m in range(1, cuts):

            @pl.when(m != n)
            def _():
                result_copy(m).wait_send()

    @pl.when(n == 0)
    def _():
        mine[...] = end_coarse[...]

    @pl.when(chain & (n > 0))
    def _():
        mine[...] = results[n]

    @pl.when(jnp.logical_not(chain) & (n > 0))
    def _():
        result_copy(n).wait_recv()

    change_ref[...] = mine[...] - end_coarse[...]
    for out in outs:
        out.wait()

    for m in range(3):

        @pl.when(n == m)
        def _():
            for copy in first_wings(m):
                copy.wait_send()

    @pl.when(jnp.logical_not(chain))
    def _():
        term_copy.wait_send()

    for which in range(2):

        @pl.when(upper | jnp.logical_not(edge[which]))
        def _():
            for copy in copies[which::2]:
                copy.wait_send()


def finish_kernel(finals, change_ref, out_u, out_v, rows):
    change = change_ref[...]
    even = even_lanes(change.shape)
    for k, (out, spread) in enumerate(
        (
            (out_u, jnp.where(even, change, pltpu.roll(change, 1, 2))),
            (out_v, jnp.where(even, pltpu.roll(change, GZ - 1, 2), change)),
        )
    ):
        for i in range(COARSE):
            slot = k * COARSE + i
            rows[slot, pl.ds(0, CY, stride=2)] = spread[i]
            rows[slot, pl.ds(1, CY, stride=2)] = spread[i]
            added = rows[slot]
            out[0, 2 * i] = finals[k, 2 * i] + added
            out[0, 2 * i + 1] = finals[k, 2 * i + 1] + added


def on_device(start_u, start_v):
    cuts = lax.axis_size("cuts")
    space = lax.axis_size("space")
    rounds = cuts // 4
    block = (COARSE, CY, GZ)
    f32 = jnp.float32
    shape = jax.ShapeDtypeStruct((1, PLANES, GY, GZ), f32)
    hbm = pl.BlockSpec(memory_space=pl.ANY)
    vmem = pl.BlockSpec(memory_space=pltpu.VMEM)
    dma = pltpu.SemaphoreType.DMA

    def body(*refs):
        kernel(cuts, space, *refs)

    finals, change = pl.pallas_call(
        body,
        out_shape=(
            jax.ShapeDtypeStruct((2, PLANES, GY, GZ), f32),
            jax.ShapeDtypeStruct(block, f32),
        ),
        in_specs=[hbm, hbm],
        out_specs=(hbm, vmem),
        scratch_shapes=[
            pltpu.VMEM((2, 2, PADDED, GY, GZ), f32),
            pltpu.VMEM((PADDED // 2, GY, GZ), f32),
            pltpu.VMEM((PADDED // 2, CY, GZ), f32),
            pltpu.VMEM(block, f32),
            pltpu.VMEM(block, f32),
            pltpu.VMEM((cuts, 16, CY, GZ), f32),
            pltpu.VMEM((rounds + 1, 20, CY, GZ), f32),
            pltpu.VMEM((cuts, *block), f32),
            dma((2,)),
            dma((4,)),
            dma((4,)),
            pltpu.SemaphoreType.REGULAR,
            dma((1,)),
            dma((cuts,)),
            dma((4,)),
            dma((cuts, 4)),
            dma((cuts, 4)),
            dma((rounds, 4)),
            dma((rounds, 4)),
            dma((cuts,)),
            dma((1,)),
        ],
        compiler_params=pltpu.CompilerParams(collective_id=0, has_side_effects=True),
        name="parareal",
    )(start_u, start_v)
    return pl.pallas_call(
        finish_kernel,
        out_shape=(shape, shape),
        in_specs=[vmem, vmem],
        out_specs=(vmem, vmem),
        scratch_shapes=[pltpu.VMEM((2 * COARSE, GY, GZ), f32)],
        name="finish",
    )(finals, change)


def solution(mesh):
    return jax.shard_map(
        on_device,
        mesh=mesh,
        in_specs=(P("cuts", "space", None, None), P("cuts", "space", None, None)),
        out_specs=(P("cuts", "space", None, None), P("cuts", "space", None, None)),
        check_vma=False,
    )
```

```python
import jax
import jax.numpy as jnp
from jax import lax
from jax.experimental import pallas as pl
from jax.experimental.pallas import tpu as pltpu
from jax.sharding import PartitionSpec as P

MESH = pl.DeviceIdType.MESH
GY = 32
GZ = 128
CY = GY // 2
PLANES = 8
COARSE = PLANES // 2
HALO = 4
PADDED = PLANES + 2 * HALO

SPREAD_FIRST = 0.14
SPREAD_SECOND = 0.13
FEED_RATE = 0.035
KILL_RATE = 0.065


def even_lanes(shape):
    return lax.broadcasted_iota(jnp.int32, shape, len(shape) - 1) % 2 == 0


def coarse_step(x):
    inner = x[1:-1]
    even = even_lanes(inner.shape)
    beside = x[2:] + x[:-2]
    beside = beside + pltpu.roll(inner, 1, 1) + pltpu.roll(inner, CY - 1, 1)
    beside = beside + pltpu.roll(inner, 2, 2) + pltpu.roll(inner, GZ - 2, 2)
    other = jnp.where(even, pltpu.roll(inner, GZ - 1, 2), pltpu.roll(inner, 1, 2))
    second = jnp.where(even, other, inner)
    feeding = inner * other * second
    spread = jnp.where(even, 0.5 * SPREAD_FIRST, 0.5 * SPREAD_SECOND)
    keep = jnp.where(
        even,
        1.0 - 3.0 * SPREAD_FIRST - 2.0 * FEED_RATE,
        1.0 - 3.0 * SPREAD_SECOND - 2.0 * (FEED_RATE + KILL_RATE),
    )
    gain = jnp.where(even, 2.0 * FEED_RATE, 0.0)
    sign = jnp.where(even, -2.0, 2.0)
    return keep * inner + spread * beside + gain + sign * feeding


def march(x):
    return coarse_step(coarse_step(x))


def fine_planes(source, target, first, count):
    def body(step, carry):
        p = first + step
        u = source[0, p]
        v = source[1, p]
        feeding = u * v * v
        beside = source[0, p - 1] + source[0, p + 1]
        beside = beside + pltpu.roll(u, 1, 0) + pltpu.roll(u, GY - 1, 0)
        beside = beside + pltpu.roll(u, 1, 1) + pltpu.roll(u, GZ - 1, 1)
        target[0, p] = (
            (1.0 - 6.0 * SPREAD_FIRST - FEED_RATE) * u + SPREAD_FIRST * beside + FEED_RATE - feeding
        )
        beside = source[1, p - 1] + source[1, p + 1]
        beside = beside + pltpu.roll(v, 1, 0) + pltpu.roll(v, GY - 1, 0)
        beside = beside + pltpu.roll(v, 1, 1) + pltpu.roll(v, GZ - 1, 1)
        target[1, p] = (
            (1.0 - 6.0 * SPREAD_SECOND - FEED_RATE - KILL_RATE) * v
            + SPREAD_SECOND * beside
            + feeding
        )
        return carry

    lax.fori_loop(0, count, body, 0, unroll=count)


def restrict(source, first, rows, out, place, count):
    def body(i, carry):
        p = first + 2 * i
        u = source[0, p] + source[0, p + 1]
        v = source[1, p] + source[1, p + 1]
        even = even_lanes(u.shape)
        rows[i] = jnp.where(even, u + pltpu.roll(u, GZ - 1, 1), v + pltpu.roll(v, 1, 1))
        out[place + i] = 0.125 * (
            rows[i, pl.ds(0, CY, stride=2)] + rows[i, pl.ds(1, CY, stride=2)]
        )
        return carry

    lax.fori_loop(0, count, body, 0, unroll=count)


def kernel(
    cuts,
    space,
    u_ref,
    v_ref,
    finals,
    change_ref,
    fine,
    rows,
    start_coarse,
    end_coarse,
    mine,
    slots,
    wides,
    results,
    load_sem,
    fine_send,
    fine_recv,
    turn,
    term_send,
    term_recv,
    first_send,
    wing_send,
    wing_recv,
    wide_send,
    wide_recv,
    result_send,
    result_recv,
):
    n = lax.axis_index("cuts")
    s = lax.axis_index("space")
    rounds = cuts // 4
    half = cuts // 2
    upper = n >= half
    row = lax.rem(s, 8)
    edge = (row == 7, row == 0)

    def at(step):
        return lax.rem(s + step + space, space)

    def seat(place):
        return lax.rem(place, 8) // 4 * 8

    chain = n == seat(s)
    barrier = pltpu.get_barrier_semaphore()

    def greet(device):
        pl.semaphore_signal(barrier, inc=1, device_id=device, device_id_type=MESH)

    def remote(source, target, send, recv, device):
        return pltpu.make_async_remote_copy(
            src_ref=source,
            dst_ref=target,
            send_sem=send,
            recv_sem=recv,
            device_id=device,
            device_id_type=MESH,
        )

    greet({"space": at(-1)})
    greet({"space": at(1)})
    @pl.when(chain)
    def _():
        for d in range(1, cuts):
            greet({"cuts": lax.rem(n + d, cuts)})
        for step in (-2, -1, 1, 2):
            greet({"cuts": seat(at(step)), "space": at(step)})
            greet({"cuts": 0, "space": at(step)})
        for m in (1, 2):
            for step in (-1, 1):
                greet({"cuts": m, "space": at(step)})

    @pl.when(jnp.logical_not(chain))
    def _():
        greet({"cuts": seat(s)})

    @pl.when(upper & (edge[0] | edge[1]))
    def _():
        greet({"cuts": n - half})

    now = fine.at[0]
    loads = []
    for k, ref in enumerate((u_ref, v_ref)):
        loads.append(
            pltpu.make_async_copy(ref.at[0], now.at[k, pl.ds(HALO, PLANES)], load_sem.at[k])
        )
    for load in loads:
        load.start()

    targets = 2 + jnp.where(chain, 4 + cuts - 1, 1)
    targets = targets + jnp.where(jnp.logical_not(upper) & (edge[0] | edge[1]), 1, 0)
    targets = targets + jnp.where(n == 0, 4, 0) + jnp.where((n == 1) | (n == 2), 2, 0)
    pl.semaphore_wait(barrier, targets)

    copies = []
    for k, ref in enumerate((u_ref, v_ref)):
        copies.append(
            remote(
                ref.at[0, pl.ds(PLANES - HALO, HALO)],
                now.at[k, pl.ds(0, HALO)],
                fine_send.at[2 * k],
                fine_recv.at[2 * k],
                {"space": at(1)},
            )
        )
        copies.append(
            remote(
                ref.at[0, pl.ds(0, HALO)],
                now.at[k, pl.ds(HALO + PLANES, HALO)],
                fine_send.at[2 * k + 1],
                fine_recv.at[2 * k + 1],
                {"space": at(-1)},
            )
        )
    def start(which):
        for copy in copies[which::2]:
            copy.start()

    for which in range(2):

        @pl.when(jnp.logical_not(upper & edge[which]))
        def _():
            start(which)

    for load in loads:
        load.wait()

    restrict(now, HALO, rows, start_coarse, 2, COARSE)
    for t in range(3):
        fine_planes(fine.at[t % 2], fine.at[(t + 1) % 2], HALO + 1 + t, PLANES - 2 - 2 * t)
    for which in range(2):

        @pl.when(upper & edge[which])
        def _():
            pl.semaphore_wait(turn, 1)
            start(which)

        @pl.when(jnp.logical_not(upper) & edge[which])
        def _():
            for copy in copies[which::2]:
                copy.wait_send()
            pl.semaphore_signal(
                turn, inc=1, device_id={"cuts": n + half}, device_id_type=MESH
            )

    for copy in copies:
        copy.wait_recv()
    restrict(now, 0, rows, start_coarse, 0, 2)
    restrict(now, HALO + PLANES, rows, start_coarse, COARSE + 2, 2)
    for t in range(3):
        source, target = fine.at[t % 2], fine.at[(t + 1) % 2]
        fine_planes(source, target, t + 1, HALO)
        fine_planes(source, target, PADDED - 1 - HALO - t, HALO)
    fine_planes(fine.at[1], fine.at[0], HALO, PLANES)
    outs = [
        pltpu.make_async_copy(now.at[k, pl.ds(HALO, PLANES)], finals.at[k], load_sem.at[k])
        for k in range(2)
    ]
    restrict(now, HALO, rows, end_coarse, 0, COARSE)
    finish = end_coarse[...]
    correction = finish - march(start_coarse[...])
    slots[n, pl.ds(6, 4)] = jnp.where(n == 0, finish, correction)

    term_copy = remote(
        slots.at[n, pl.ds(6, 4)],
        slots.at[n, pl.ds(6, 4)],
        term_send.at[0],
        term_recv.at[n],
        {"cuts": seat(s)},
    )

    def wing_copy(m, source, target, width, step, side, send):
        return remote(
            slots.at[m, pl.ds(6 + source, width)],
            slots.at[m, pl.ds(target, width)],
            send,
            wing_recv.at[m, side],
            {"cuts": seat(at(step)), "space": at(step)},
        )

    wings = (
        ((2, 0, 2, 2, 2), (0, 14, 2, -2, 3), (0, 2, 4, 1, 0), (0, 10, 4, -1, 1)),
        ((0, 2, 4, 1, 0), (0, 10, 4, -1, 1)),
        ((2, 4, 2, 1, 0), (0, 10, 2, -1, 1)),
    )

    def first_wings(m):
        return [wing_copy(m, *wing, first_send.at[wing[4]]) for wing in wings[m]]

    def later_wings(m, kind):
        return [wing_copy(m, *wing, wing_send.at[m, wing[4]]) for wing in wings[kind]]

    for m in range(3):

        @pl.when(n == m)
        def _():
            for copy in first_wings(m):
                copy.start()

    @pl.when(jnp.logical_not(chain))
    def _():
        term_copy.start()

    for out in outs:
        out.start()

    def await_term(m):
        @pl.when(n != m)
        def _():
            own = slots.at[m, pl.ds(6, 4)]
            remote(own, own, term_send.at[0], term_recv.at[m], {"space": at(1)}).wait_recv()

    def result_copy(m):
        return remote(
            results.at[m], mine, result_send.at[m], result_recv.at[0], {"cuts": m}
        )

    def deliver(m, state):
        results[m] = state

        @pl.when(m != n)
        def _():
            result_copy(m).start()

    def wide_copies(r):
        return [
            remote(
                wides.at[r, pl.ds(8, 4)],
                wides.at[r, pl.ds(target, 4)],
                wide_send.at[r, side],
                wide_recv.at[r, side],
                {"cuts": seat(at(step)), "space": at(step)},
            )
            for target, step, side in ((0, 2, 2), (16, -2, 3), (4, 1, 0), (12, -1, 1))
        ]

    def forward(base):
        for kind in range(3):
            await_term(base + kind)
            for copy in later_wings(base + kind, kind):
                copy.start()

    def three_links(base, wide, r, arrive):
        wide = march(wide)
        arrive(1)
        wide = wide + slots[base + 1, 2:14]
        deliver(base + 1, wide[4:8])
        wide = march(wide)
        arrive(2)
        wide = wide + slots[base + 2, 4:12]
        deliver(base + 2, wide[2:6])
        wide = march(wide)
        await_term(base + 3)
        state = wide + slots[base + 3, 6:10]
        wides[r + 1, pl.ds(8, 4)] = state

        @pl.when(r < rounds - 1)
        def _():
            for copy in wide_copies(r + 1):
                copy.start()
            forward(base + 4)

        deliver(base + 3, state)

    @pl.when(chain)
    def _():
        def arrive_first(m):
            await_term(m)
            for copy in first_wings(m):
                copy.wait_recv()

        arrive_first(0)
        three_links(0, slots[0], 0, arrive_first)

        def one_round(r, carry):
            base = 4 * r

            def arrive(kind):
                for copy in later_wings(base + kind, kind):
                    copy.wait()

            for copy in wide_copies(r):
                copy.wait()
            wide = march(wides[r])
            arrive(0)
            wide = wide + slots[base]
            deliver(base, wide[6:10])
            three_links(base, wide, r, arrive)
            return carry

        lax.fori_loop(1, rounds, one_round, 0)
        for m in range(1, cuts):

            @pl.when(m != n)
            def _():
                result_copy(m).wait_send()

    @pl.when(n == 0)
    def _():
        mine[...] = end_coarse[...]

    @pl.when(chain & (n > 0))
    def _():
        mine[...] = results[n]

    @pl.when(jnp.logical_not(chain) & (n > 0))
    def _():
        result_copy(n).wait_recv()

    change_ref[...] = mine[...] - end_coarse[...]
    for out in outs:
        out.wait()

    for m in range(3):

        @pl.when(n == m)
        def _():
            for copy in first_wings(m):
                copy.wait_send()

    @pl.when(jnp.logical_not(chain))
    def _():
        term_copy.wait_send()

    for which in range(2):

        @pl.when(upper | jnp.logical_not(edge[which]))
        def _():
            for copy in copies[which::2]:
                copy.wait_send()


def finish_kernel(finals, change_ref, out_u, out_v, rows):
    change = change_ref[...]
    even = even_lanes(change.shape)
    for k, (out, spread) in enumerate(
        (
            (out_u, jnp.where(even, change, pltpu.roll(change, 1, 2))),
            (out_v, jnp.where(even, pltpu.roll(change, GZ - 1, 2), change)),
        )
    ):
        for i in range(COARSE):
            slot = k * COARSE + i
            rows[slot, pl.ds(0, CY, stride=2)] = spread[i]
            rows[slot, pl.ds(1, CY, stride=2)] = spread[i]
            added = rows[slot]
            out[0, 2 * i] = finals[k, 2 * i] + added
            out[0, 2 * i + 1] = finals[k, 2 * i + 1] + added


def on_device(start_u, start_v):
    cuts = lax.axis_size("cuts")
    space = lax.axis_size("space")
    rounds = cuts // 4
    block = (COARSE, CY, GZ)
    f32 = jnp.float32
    shape = jax.ShapeDtypeStruct((1, PLANES, GY, GZ), f32)
    hbm = pl.BlockSpec(memory_space=pl.ANY)
    vmem = pl.BlockSpec(memory_space=pltpu.VMEM)
    dma = pltpu.SemaphoreType.DMA

    def body(*refs):
        kernel(cuts, space, *refs)

    finals, change = pl.pallas_call(
        body,
        out_shape=(
            jax.ShapeDtypeStruct((2, PLANES, GY, GZ), f32),
            jax.ShapeDtypeStruct(block, f32),
        ),
        in_specs=[hbm, hbm],
        out_specs=(hbm, vmem),
        scratch_shapes=[
            pltpu.VMEM((2, 2, PADDED, GY, GZ), f32),
            pltpu.VMEM((PADDED // 2, GY, GZ), f32),
            pltpu.VMEM((PADDED // 2, CY, GZ), f32),
            pltpu.VMEM(block, f32),
            pltpu.VMEM(block, f32),
            pltpu.VMEM((cuts, 16, CY, GZ), f32),
            pltpu.VMEM((rounds + 1, 20, CY, GZ), f32),
            pltpu.VMEM((cuts, *block), f32),
            dma((2,)),
            dma((4,)),
            dma((4,)),
            pltpu.SemaphoreType.REGULAR,
            dma((1,)),
            dma((cuts,)),
            dma((4,)),
            dma((cuts, 4)),
            dma((cuts, 4)),
            dma((rounds, 4)),
            dma((rounds, 4)),
            dma((cuts,)),
            dma((1,)),
        ],
        compiler_params=pltpu.CompilerParams(collective_id=0, has_side_effects=True),
        name="parareal",
    )(start_u, start_v)
    return pl.pallas_call(
        finish_kernel,
        out_shape=(shape, shape),
        in_specs=[vmem, vmem],
        out_specs=(vmem, vmem),
        scratch_shapes=[pltpu.VMEM((2 * COARSE, GY, GZ), f32)],
        name="finish",
    )(finals, change)


def solution(mesh):
    return jax.shard_map(
        on_device,
        mesh=mesh,
        in_specs=(P("cuts", "space", None, None), P("cuts", "space", None, None)),
        out_specs=(P("cuts", "space", None, None), P("cuts", "space", None, None)),
        check_vma=False,
    )
```
